128 devices in a mesh: packs: 8 (over x, core), seq: 16 (over y, z).
Axes of the slice: x: 4, y: 4, z: 4, core: 2. Of those that a mesh axis runs over, the one named last changes fastest.
Arguments:
- queries: bfloat16 [16384, 8192], P(('packs', 'seq')), parts along dimension 0, may hold values from -12 to 12
- keys: bfloat16 [16384, 1024], P(('packs', 'seq')), parts along dimension 0, may hold values from -6 to 6
- values: bfloat16 [16384, 1024], P(('packs', 'seq')), parts along dimension 0, may hold values from -6 to 6
- outputs: bfloat16 [16384, 8192], P(('packs', 'seq')), parts along dimension 0, may hold values from -6 to 6
- grad_out: bfloat16 [16384, 8192], P(('packs', 'seq')), parts along dimension 0, may hold values from -4 to 4
- lse_saved: float32 [16384, 64], P(('packs', 'seq')), parts along dimension 0, may hold values from -40 to 40, as said below
- doc_lengths: int32 [64], P('packs'), parts along dimension 0, may hold values from 1 to 1024, as said below
Outputs:
- grad_queries: bfloat16 [16384, 8192], P(('packs', 'seq')), parts along dimension 0
- grad_keys: bfloat16 [16384, 1024], P(('packs', 'seq')), parts along dimension 0
- grad_values: bfloat16 [16384, 1024], P(('packs', 'seq')), parts along dimension 0
The draws below stay inside these ranges and needn't reach their ends.
There are 8 independent parts, one for each index of `packs`. The reference program is written for one: setup_inputs(seed, part) draws one part's arguments, and reference() takes and returns one part's arrays. A program takes and returns all parts, laid end to end along the dimension named above; each array names one. Nothing has to cross between parts.
Inputs may be any that keep to these rules, and one draw needn't show every extreme that they name: `doc_lengths`: positive lengths summing to 2048; one document has exactly 1024 tokens. lse_saved is the log-sum-exp over visible keys of the scores of queries and keys as defined in the reference program, for every row and head.
All inputs are finite; a program needn't handle non-finite values.
Results may differ from the reference program's by a relative error of at most 0.0049.
Values may be sent and summed in bfloat16 or wider, within the bound.
A program may use at most 64 MiB of HBM per device.

```python
import jax
import jax.numpy as jnp
from jax import lax

HEADS = 64
KVH = 8
HDIM = 128
DOCS = 8
TOKENS = 2048
MOST = 1024


def draw_doc_lengths(key, part):
    rest = TOKENS - MOST
    weights = jax.random.randint(jax.random.fold_in(key, 11), (DOCS - 1,), 1, 9).astype(jnp.int32)
    shares = weights * rest // jnp.sum(weights)
    shares = shares.at[0].add(rest - jnp.sum(shares))
    lengths = jnp.concatenate([jnp.full((1,), MOST, dtype=jnp.int32), shares.astype(jnp.int32)])
    offset = jax.random.randint(jax.random.fold_in(key, 12), (), 0, DOCS)
    return jnp.roll(lengths, offset).astype(jnp.int32)


def raw_queries(key):
    drawn = jnp.clip(jax.random.normal(jax.random.fold_in(key, 21), (TOKENS, HEADS * HDIM), jnp.float32), -6.0, 6.0)
    return drawn


def raw_keys(key):
    return jnp.clip(jax.random.normal(jax.random.fold_in(key, 23), (TOKENS, KVH * HDIM), jnp.float32), -6.0, 6.0)


def draw_queries(key, part):
    return raw_queries(key).astype(jnp.bfloat16)


def draw_keys(key, part):
    return raw_keys(key).astype(jnp.bfloat16)


def draw_lse_saved(key, part):
    total = TOKENS
    scale = 1.0 / HDIM ** 0.5
    group = HEADS // KVH
    query_heads = raw_queries(key).astype(jnp.bfloat16).astype(jnp.float32).reshape(total, HEADS, HDIM)
    key_heads = raw_keys(key).astype(jnp.bfloat16).astype(jnp.float32).reshape(total, KVH, HDIM)
    lengths = draw_doc_lengths(key, part)
    boundary = jnp.cumsum(lengths)
    position = jnp.arange(total, dtype=jnp.int32)
    segment = jnp.sum((position[:, None] >= boundary[None, :]).astype(jnp.int32), axis=1)
    visible = (position[None, :] <= position[:, None]) & (segment[None, :] == segment[:, None])

    def one_head(head):
        query_one = lax.dynamic_index_in_dim(query_heads, head, 1, keepdims=False)
        key_one = lax.dynamic_index_in_dim(key_heads, head // group, 1, keepdims=False)
        scores = jnp.dot(query_one, key_one.T, precision=lax.Precision.HIGHEST) * scale
        return jax.nn.logsumexp(jnp.where(visible, scores, -jnp.inf), axis=1)
    return lax.map(one_head, jnp.arange(HEADS, dtype=jnp.int32)).T.astype(jnp.float32)


def shard_levels(own_key, shape, pieces, low, top_value):
    factor_of, own = 1.0, jax.random.fold_in(own_key, 6)
    for dim, parts in pieces:
        draws = jnp.exp(jax.random.uniform(jax.random.fold_in(own, dim), (parts,), jnp.float32, low / len(pieces), top_value / len(pieces)))
        factor_of = factor_of * jnp.repeat(draws, shape[dim] // parts).reshape([-1 if axis == dim else 1 for axis in range(len(shape))])
    return factor_of


def gaussian(stream_key, extent, spread, bound, pieces=(), kind=jnp.bfloat16):
    entries = jax.random.normal(stream_key, extent, jnp.float32) * spread
    if len(pieces) > 0:
        entries = shard_levels(stream_key, extent, pieces, -0.22, 0.18) * entries
    return jnp.clip(entries, min=-bound, max=bound).astype(kind)


def setup_inputs(seed: int = 0, part: int = 0) -> dict:
    seeds = jax.random.split(jax.random.key(seed), 8)
    own_keys = jax.random.split(jax.random.fold_in(seeds[7], part), 8)
    return {
        "queries": draw_queries(jax.random.fold_in(jax.random.fold_in(seeds[7], part), 71), part),
        "keys": draw_keys(jax.random.fold_in(jax.random.fold_in(seeds[7], part), 71), part),
        "values": gaussian(own_keys[2], (TOKENS, KVH * HDIM), 1.0, 6.0, ((0, 16),)),
        "outputs": gaussian(own_keys[3], (TOKENS, HEADS * HDIM), 1.0, 6.0, ((0, 16),)),
        "grad_out": gaussian(own_keys[4], (TOKENS, HEADS * HDIM), 0.3, 4.0, ((0, 16),)),
        "lse_saved": draw_lse_saved(jax.random.fold_in(jax.random.fold_in(seeds[7], part), 71), part),
        "doc_lengths": draw_doc_lengths(jax.random.fold_in(jax.random.fold_in(seeds[7], part), 71), part),
    }


def segment_ids(doc_lengths, total):
    boundary = jnp.cumsum(doc_lengths)
    position = jnp.arange(total, dtype=jnp.int32)
    return jnp.sum((position[:, None] >= boundary[None, :]).astype(jnp.int32), axis=1)


def reference(queries, keys, values, outputs, grad_out, lse_saved, doc_lengths):
    total = TOKENS
    scale = 1.0 / (HDIM ** 0.5)
    group = HEADS // KVH
    segment = segment_ids(doc_lengths, total)
    position = jnp.arange(total, dtype=jnp.int32)
    visible = (position[None, :] <= position[:, None]) & (segment[None, :] == segment[:, None])
    query_heads = queries.reshape(total, HEADS, HDIM)
    gout_heads = grad_out.reshape(total, HEADS, HDIM)
    out_heads = outputs.reshape(total, HEADS, HDIM)
    key_heads = keys.reshape(total, KVH, HDIM)
    value_heads = values.reshape(total, KVH, HDIM)
    delta = jnp.sum(out_heads.astype(jnp.float32) * gout_heads.astype(jnp.float32), axis=2)

    def one_head(head):
        kv_index = head // group
        query_one = lax.dynamic_index_in_dim(query_heads, head, 1, keepdims=False)
        gout_one = lax.dynamic_index_in_dim(gout_heads, head, 1, keepdims=False)
        key_one = lax.dynamic_index_in_dim(key_heads, kv_index, 1, keepdims=False)
        value_one = lax.dynamic_index_in_dim(value_heads, kv_index, 1, keepdims=False)
        lse_one = lax.dynamic_index_in_dim(lse_saved, head, 1, keepdims=False)
        delta_one = lax.dynamic_index_in_dim(delta, head, 1, keepdims=False)
        scores = jnp.dot(query_one, key_one.T, preferred_element_type=jnp.float32) * scale
        attn_prob = jnp.where(visible, jnp.exp(scores - lse_one[:, None]), 0.0)
        grad_prob = jnp.dot(gout_one, value_one.T, preferred_element_type=jnp.float32)
        grad_score = (attn_prob * (grad_prob - delta_one[:, None])).astype(jnp.bfloat16)
        prob_half = attn_prob.astype(jnp.bfloat16)
        grad_query = (jnp.dot(grad_score, key_one, preferred_element_type=jnp.float32) * scale).astype(jnp.bfloat16)
        grad_key = jnp.dot(grad_score.T, query_one, preferred_element_type=jnp.float32) * scale
        grad_value = jnp.dot(prob_half.T, gout_one, preferred_element_type=jnp.float32)
        return grad_query, grad_key, grad_value

    grad_q_all, grad_k_all, grad_v_all = lax.map(one_head, jnp.arange(HEADS, dtype=jnp.int32))
    grad_queries = jnp.transpose(grad_q_all, (1, 0, 2)).reshape(total, HEADS * HDIM)
    grad_keys = jnp.sum(grad_k_all.reshape(KVH, group, total, HDIM), axis=1)
    grad_values = jnp.sum(grad_v_all.reshape(KVH, group, total, HDIM), axis=1)
    grad_keys = jnp.transpose(grad_keys, (1, 0, 2)).reshape(total, KVH * HDIM).astype(jnp.bfloat16)
    grad_values = jnp.transpose(grad_values, (1, 0, 2)).reshape(total, KVH * HDIM).astype(jnp.bfloat16)
    return grad_queries, grad_keys, grad_values
```

```python
import functools

import jax
import jax.numpy as jnp
from jax import lax
from jax.experimental import pallas as pl
from jax.experimental.pallas import tpu as pltpu
from jax.sharding import PartitionSpec as P

HEADS = 64
KVH = 8
HDIM = 128
GROUP = HEADS // KVH
ROWS = 128
WIDE = GROUP * HDIM
SIDE = 4
SLOTS = 9
KEYS = SLOTS * ROWS
DOCS = 8
SCALE = 1.0 / HDIM**0.5
LOG2E = 1.4426950408889634
MESH = pl.DeviceIdType.MESH


def kernel(
    q_hbm,
    k_hbm,
    v_hbm,
    o_hbm,
    go_hbm,
    lse_ref,
    doc_ref,
    gq_hbm,
    gk_ref,
    gv_ref,
    kvw,
    part,
    own,
    outr,
    sums,
    yr,
    qb,
    gb,
    ob,
    gqb,
    qs,
    gs,
    lse_t,
    nlse,
    delta,
    bias,
    in_sem,
    kv_sem,
    out_sem,
    send_sem,
    recv_sem,
):
    me = lax.axis_index("seq")
    y, z = me // SIDE, lax.rem(me, SIDE)

    def at(dy, dz):
        return lax.rem(y + dy + SIDE, SIDE) * SIDE + lax.rem(z + dz + SIDE, SIDE)

    def remote(src, dst, kind, g, target):
        return pltpu.make_async_remote_copy(
            src_ref=src,
            dst_ref=dst,
            send_sem=send_sem.at[kind, g],
            recv_sem=recv_sem.at[kind, g],
            device_id={"seq": target},
            device_id_type=MESH,
        )

    up_first = jnp.where(z == 3, 1, 0)
    down_first = jnp.where(z == 0, 0, 1)
    relay_up = jnp.where(z == 3, 4, 3)
    relay_down = jnp.where(z == 0, 7, 8)

    def y_in(j, g):
        return remote(kvw.at[:, g, 0], kvw.at[:, g, j], j - 1, g, at(j, 0))

    def z_up(g):
        return remote(kvw.at[:, g, pl.ds(up_first, 2)], kvw.at[:, g, pl.ds(3, 2)], 2, g, at(0, 1))

    def z_down(g):
        return remote(
            kvw.at[:, g, pl.ds(down_first, 2)], kvw.at[:, g, pl.ds(7, 2)], 3, g, at(0, -1)
        )

    def far_up(g):
        return remote(kvw.at[:, g, relay_up], kvw.at[:, g, 5], 4, g, at(0, 1))

    def far_down(g):
        return remote(kvw.at[:, g, relay_down], kvw.at[:, g, 6], 5, g, at(0, -1))

    def z_out(d, g):
        return remote(part.at[:, g, pl.ds(2 * d - 2, 2)], outr.at[d - 1, :, g], 5 + d, g, at(0, -d))

    def y_out(j, g):
        return remote(sums.at[:, g, j - 1], yr.at[j - 1, :, g], 8 + j, g, at(-j, 0))

    def columns(g, width):
        return pl.ds(pl.multiple_of(g * width, width), width)

    def load_kv(n, g):
        src = (k_hbm, v_hbm)[n]
        return pltpu.make_async_copy(
            src.at[:, columns(g, HDIM)], kvw.at[n, g, 0], kv_sem.at[n, g]
        )

    def load_wide(n, g):
        src, dst = ((q_hbm, qb), (go_hbm, gb), (o_hbm, ob))[n]
        return pltpu.make_async_copy(src.at[:, columns(g, WIDE)], dst.at[g], in_sem.at[n, g])

    def store_wide(g):
        return pltpu.make_async_copy(gqb.at[g], gq_hbm.at[:, columns(g, WIDE)], out_sem.at[g])

    for g in range(KVH):
        load_kv(0, g).start()
        load_kv(1, g).start()
    for g in range(KVH):
        for n in range(3):
            load_wide(n, g).start()

    barrier = pltpu.get_barrier_semaphore()
    for dy, dz in ((1, 0), (2, 0), (3, 0), (0, 1), (0, 2), (0, 3)):
        pl.semaphore_signal(
            barrier, inc=1, device_id={"seq": at(dy, dz)}, device_id_type=MESH
        )
    pl.semaphore_wait(barrier, 6)

    for g in range(KVH):
        load_kv(0, g).wait()
        load_kv(1, g).wait()
        y_in(1, g).start()
        y_in(2, g).start()

    lse_t[...] = lse_ref[...].T * LOG2E
    time = lax.broadcasted_iota(jnp.int32, (1, ROWS), 1) + me * ROWS
    begin = jnp.zeros((1, ROWS), jnp.int32)
    bound = doc_ref[0]
    for n in range(1, DOCS):
        begin = jnp.where(time >= bound, bound, begin)
        bound = bound + doc_ref[n]
    for slot in range(SLOTS):
        if slot < 3:
            row, col = at(-slot, 0), 0
        else:
            d, second = (slot - 3) // 2 + 1, (slot - 3) % 2
            wrapped = jnp.where(z >= d, 0, 1)
            row = lax.rem(y - wrapped - second + SIDE, SIDE) * SIDE + lax.rem(z - d + SIDE, SIDE)
        keys_at = lax.broadcasted_iota(jnp.int32, (ROWS, ROWS), 0) + row * ROWS
        seen = (keys_at <= time) & (keys_at >= begin)
        bias[pl.ds(slot * ROWS, ROWS), :] = jnp.where(seen, 0.0, -1e30)

    def compute(g):
        for n in range(3):
            load_wide(n, g).wait()
        logs = lse_t[pl.ds(pl.multiple_of(g * GROUP, GROUP), GROUP), :]
        for h in range(GROUP):
            cut = slice(h * HDIM, (h + 1) * HDIM)
            query, gout = qb[g, :, cut], gb[g, :, cut]
            qs[cut, :] = query
            gs[cut, :] = gout
            product = ob[g, :, cut].astype(jnp.float32) * gout.astype(jnp.float32)
            delta[:, cut] = jnp.sum(product.T, axis=0, keepdims=True)
            nlse[:, cut] = logs[h : h + 1, :]
        k = kvw[0, g].reshape(KEYS, HDIM)
        v = kvw[1, g].reshape(KEYS, HDIM)
        nt = (((1,), (1,)), ((), ()))
        tn = (((0,), (0,)), ((), ()))
        scores = lax.dot_general(k, qs[...], nt, preferred_element_type=jnp.float32)
        hidden = jnp.concatenate([bias[...]] * GROUP, axis=1)
        prob = jnp.exp2(scores * (SCALE * LOG2E) - nlse[...] + hidden)
        grad_prob = lax.dot_general(v, gs[...], nt, preferred_element_type=jnp.float32)
        grad_score = (prob * (grad_prob - delta[...])).astype(jnp.bfloat16)
        half = prob.astype(jnp.bfloat16)
        grad_v = jnp.dot(half, gs[...], preferred_element_type=jnp.float32)
        grad_k = jnp.dot(grad_score, qs[...], preferred_element_type=jnp.float32) * SCALE
        near = 3 * ROWS
        for n, grad in ((0, grad_k), (1, grad_v)):
            own[n, g] = grad[:near].reshape(3, ROWS, HDIM)
            part[n, g] = grad[near:].reshape(6, ROWS, HDIM).astype(jnp.bfloat16)
        grad_q = lax.dot_general(k, grad_score, tn, preferred_element_type=jnp.float32)
        for h in range(GROUP):
            cut = slice(h * HDIM, (h + 1) * HDIM)
            gqb[g, :, cut] = (grad_q[:, cut].T * SCALE).astype(jnp.bfloat16)
        store_wide(g).start()

    def step(s, carry):
        @pl.when(s < KVH)
        def _():
            y_in(1, s).wait_recv()
            y_in(2, s).wait_recv()
            z_up(s).start()
            z_down(s).start()

        @pl.when((s >= 1) & (s < KVH + 1))
        def _():
            g = s - 1
            z_up(g).wait_recv()
            z_down(g).wait_recv()
            far_up(g).start()
            far_down(g).start()

        @pl.when((s >= 2) & (s < KVH + 2))
        def _():
            g = s - 2
            far_up(g).wait_recv()
            far_down(g).wait_recv()
            compute(g)
            for d in (1, 2, 3):
                z_out(d, g).start()

        @pl.when((s >= 3) & (s < KVH + 3))
        def _():
            g = s - 3
            for d in (1, 2, 3):
                z_out(d, g).wait_recv()
                first = jnp.where(z + d < SIDE, 0, 1)
                for n in range(2):
                    own[n, g, pl.ds(first, 2)] += outr[d - 1, n, g].astype(jnp.float32)
            for n in range(2):
                sums[n, g] = own[n, g, pl.ds(1, 2)].astype(jnp.bfloat16)
            y_out(1, g).start()
            y_out(2, g).start()

        @pl.when(s >= 4)
        def _():
            g = s - 4
            y_out(1, g).wait_recv()
            y_out(2, g).wait_recv()
            for n, ref in ((0, gk_ref), (1, gv_ref)):
                total = (
                    own[n, g, 0]
                    + yr[0, n, g].astype(jnp.float32)
                    + yr[1, n, g].astype(jnp.float32)
                )
                ref[:, columns(g, HDIM)] = total.astype(jnp.bfloat16)

        return carry

    lax.fori_loop(0, KVH + 4, step, 0)

    def drain(g, carry):
        y_in(1, g).wait_send()
        y_in(2, g).wait_send()
        z_up(g).wait_send()
        z_down(g).wait_send()
        far_up(g).wait_send()
        far_down(g).wait_send()
        for d in (1, 2, 3):
            z_out(d, g).wait_send()
        y_out(1, g).wait_send()
        y_out(2, g).wait_send()
        store_wide(g).wait()
        return carry

    lax.fori_loop(0, KVH, drain, 0)


def shards(queries, keys, values, outputs, grad_out, lse_saved, doc_lengths):
    half, full = jnp.bfloat16, jnp.float32
    anywhere = pl.BlockSpec(memory_space=pl.ANY)
    vmem = pl.BlockSpec(memory_space=pltpu.VMEM)
    return pl.pallas_call(
        kernel,
        out_shape=(
            jax.ShapeDtypeStruct((ROWS, HEADS * HDIM), half),
            jax.ShapeDtypeStruct((ROWS, KVH * HDIM), half),
            jax.ShapeDtypeStruct((ROWS, KVH * HDIM), half),
        ),
        in_specs=[anywhere] * 5 + [vmem, pl.BlockSpec(memory_space=pltpu.SMEM)],
        out_specs=(anywhere, vmem, vmem),
        scratch_shapes=[
            pltpu.VMEM((2, KVH, SLOTS, ROWS, HDIM), half),
            pltpu.VMEM((2, KVH, 6, ROWS, HDIM), half),
            pltpu.VMEM((2, KVH, 3, ROWS, HDIM), full),
            pltpu.VMEM((3, 2, KVH, 2, ROWS, HDIM), half),
            pltpu.VMEM((2, KVH, 2, ROWS, HDIM), half),
            pltpu.VMEM((2, 2, KVH, ROWS, HDIM), half),
            pltpu.VMEM((KVH, ROWS, WIDE), half),
            pltpu.VMEM((KVH, ROWS, WIDE), half),
            pltpu.VMEM((KVH, ROWS, WIDE), half),
            pltpu.VMEM((KVH, ROWS, WIDE), half),
            pltpu.VMEM((WIDE, HDIM), half),
            pltpu.VMEM((WIDE, HDIM), half),
            pltpu.VMEM((HEADS, ROWS), full),
            pltpu.VMEM((1, WIDE), full),
            pltpu.VMEM((1, WIDE), full),
            pltpu.VMEM((KEYS, ROWS), full),
            pltpu.SemaphoreType.DMA((3, KVH)),
            pltpu.SemaphoreType.DMA((2, KVH)),
            pltpu.SemaphoreType.DMA((KVH,)),
            pltpu.SemaphoreType.DMA((11, KVH)),
            pltpu.SemaphoreType.DMA((11, KVH)),
        ],
        compiler_params=pltpu.CompilerParams(
            collective_id=0,
            has_side_effects=True,
            vmem_limit_bytes=62 * 1024 * 1024,
        ),
        name="attention_backward",
    )(queries, keys, values, outputs, grad_out, lse_saved, doc_lengths)


def solution(mesh):
    placed = P(("packs", "seq"), None)
    return jax.shard_map(
        shards,
        mesh=mesh,
        in_specs=(placed,) * 6 + (P("packs"),),
        out_specs=(placed,) * 3,
        check_vma=False,
    )
```

```python
import functools

import jax
import jax.numpy as jnp
from jax import lax
from jax.experimental import pallas as pl
from jax.experimental.pallas import tpu as pltpu
from jax.sharding import PartitionSpec as P

HEADS = 64
KVH = 8
HDIM = 128
GROUP = HEADS // KVH
ROWS = 128
WIDE = GROUP * HDIM
SIDE = 4
SLOTS = 9
KEYS = SLOTS * ROWS
DOCS = 8
LAG = (1, 2, 3, 4, 5)
SCALE = 1.0 / HDIM**0.5
LOG2E = 1.4426950408889634
MESH = pl.DeviceIdType.MESH


def kernel(
    q_hbm,
    k_hbm,
    v_hbm,
    o_hbm,
    go_hbm,
    lse_ref,
    doc_ref,
    gq_hbm,
    gk_ref,
    gv_ref,
    kvw,
    part,
    acc,
    partr,
    cross,
    crossr,
    side,
    sider,
    prev,
    prevr,
    qb,
    gb,
    ob,
    gqb,
    qs,
    gs,
    lse_t,
    nlse,
    delta,
    bias,
    in_sem,
    kv_sem,
    out_sem,
    send_sem,
    recv_sem,
):
    me = lax.axis_index("seq")
    y, z = me // SIDE, lax.rem(me, SIDE)

    def at(dy, dz):
        return lax.rem(y + dy + SIDE, SIDE) * SIDE + lax.rem(z + dz + SIDE, SIDE)

    def remote(src, dst, kind, g, target):
        return pltpu.make_async_remote_copy(
            src_ref=src,
            dst_ref=dst,
            send_sem=send_sem.at[kind, g],
            recv_sem=recv_sem.at[kind, g],
            device_id={"seq": target},
            device_id_type=MESH,
        )

    firsts = (jnp.where(z < 3, 0, 1), jnp.where(z < 2, 0, 1), jnp.where(z < 1, 0, 1))

    def y_in(j, g):
        return remote(kvw.at[:, g, j - 1], kvw.at[:, g, j], j - 1, g, at(1, 0))

    def z_in(d, g):
        return remote(kvw.at[:, g, firsts[d - 1]], kvw.at[:, g, 2 + d], 1 + d, g, at(0, d))

    second = firsts[0] + 1

    def k_in(g):
        return remote(kvw.at[0, g, second], kvw.at[0, g, 6], 5, g, at(0, 1))

    def row_in(n, g):
        return remote(
            kvw.at[n, g, pl.ds(4 - n, 2 + n)], kvw.at[n, g, pl.ds(7 - n, 2 + n)], 6 + n, g, at(1, 0)
        )

    def row_out(n, g):
        rows = pl.ds(1 - n, 2 + n)
        return remote(part.at[n, g, rows], partr.at[n, g, rows], 8 + n, g, at(-1, 0))

    def k_out(g):
        return remote(cross.at[g], crossr.at[g], 10, g, at(0, -1))

    def z_out(d, g):
        return remote(side.at[:, g, d - 1], sider.at[d - 1, :, g], 10 + d, g, at(0, -d))

    def y_out(j, g):
        return remote(prev.at[:, g, j], prevr.at[:, g, j], 14 + j, g, at(-1, 0))

    def columns(g, width):
        return pl.ds(pl.multiple_of(g * width, width), width)

    def load_kv(n, g):
        src = (k_hbm, v_hbm)[n]
        return pltpu.make_async_copy(
            src.at[:, columns(g, HDIM)], kvw.at[n, g, 0], kv_sem.at[n, g]
        )

    def load_wide(n, g):
        src, dst = ((q_hbm, qb), (go_hbm, gb), (o_hbm, ob))[n]
        return pltpu.make_async_copy(src.at[:, columns(g, WIDE)], dst.at[g], in_sem.at[n, g])

    def store_wide(g):
        return pltpu.make_async_copy(gqb.at[g], gq_hbm.at[:, columns(g, WIDE)], out_sem.at[g])

    for g in range(KVH):
        load_kv(0, g).start()
        load_kv(1, g).start()
    for g in range(KVH):
        for n in range(3):
            load_wide(n, g).start()

    barrier = pltpu.get_barrier_semaphore()
    for dy, dz in ((1, 0), (2, 0), (3, 0), (0, 1), (0, 2), (0, 3)):
        pl.semaphore_signal(
            barrier, inc=1, device_id={"seq": at(dy, dz)}, device_id_type=MESH
        )
    pl.semaphore_wait(barrier, 6)

    def send_first(g):
        load_kv(0, g).wait()
        load_kv(1, g).wait()
        y_in(1, g).start()

    send_first(0)
    send_first(1)

    lse_t[...] = lse_ref[...] * LOG2E
    time = lax.broadcasted_iota(jnp.int32, (1, ROWS), 1) + me * ROWS
    begin = jnp.zeros((1, ROWS), jnp.int32)
    bound = doc_ref[0]
    for n in range(1, DOCS):
        begin = jnp.where(time >= bound, bound, begin)
        bound = bound + doc_ref[n]
    for slot in range(SLOTS):
        back = (0, 4, 8, 1, 2, 3, 5, 6, 7)[slot]
        row = lax.rem(me - back + SIDE * SIDE, SIDE * SIDE)
        keys_at = lax.broadcasted_iota(jnp.int32, (ROWS, ROWS), 0) + row * ROWS
        seen = (keys_at <= time) & (keys_at >= begin)
        bias[pl.ds(slot * ROWS, ROWS), :] = jnp.where(seen, 0.0, -1e30)

    def compute(g):
        for n in range(3):
            load_wide(n, g).wait()
        logs = lse_t[pl.ds(pl.multiple_of(g * GROUP, GROUP), GROUP), :]
        for h in range(GROUP):
            cut = slice(h * HDIM, (h + 1) * HDIM)
            query, gout = qb[g, :, cut], gb[g, :, cut]
            qs[cut, :] = query
            gs[cut, :] = gout
            product = ob[g, :, cut].astype(jnp.float32) * gout.astype(jnp.float32)
            delta[:, cut] = jnp.sum(product.T, axis=0, keepdims=True)
            nlse[:, cut] = logs[h : h + 1, :]
        k = kvw[0, g].reshape(KEYS, HDIM)
        v = kvw[1, g].reshape(KEYS, HDIM)
        nt = (((1,), (1,)), ((), ()))
        tn = (((0,), (0,)), ((), ()))
        scores = lax.dot_general(k, qs[...], nt, preferred_element_type=jnp.float32)
        hidden = jnp.concatenate([bias[...]] * GROUP, axis=1)
        prob = jnp.exp2(scores * (SCALE * LOG2E) - nlse[...] + hidden)
        grad_prob = lax.dot_general(v, gs[...], nt, preferred_element_type=jnp.float32)
        grad_score = (prob * (grad_prob - delta[...])).astype(jnp.bfloat16)
        half = prob.astype(jnp.bfloat16)
        grad_v = jnp.dot(half, gs[...], preferred_element_type=jnp.float32)
        grad_k = jnp.dot(grad_score, qs[...], preferred_element_type=jnp.float32) * SCALE
        for n, grad in ((0, grad_k), (1, grad_v)):
            tile = grad.reshape(SLOTS, ROWS, HDIM)
            acc[n, g] = tile[0:6]
            part[n, g] = tile[6:9].astype(jnp.bfloat16)
        cross[g] = part[0, g, 0]
        grad_q = lax.dot_general(k, grad_score, tn, preferred_element_type=jnp.float32)
        for h in range(GROUP):
            cut = slice(h * HDIM, (h + 1) * HDIM)
            gqb[g, :, cut] = (grad_q[:, cut].T * SCALE).astype(jnp.bfloat16)
        store_wide(g).start()

    def step(s, carry):
        @pl.when(s < KVH)
        def _():
            y_in(1, s).wait_recv()
            for d in (1, 2, 3):
                z_in(d, s).start()
            y_in(2, s).start()

            @pl.when(s < KVH - 2)
            def _():
                send_first(s + 2)

        @pl.when((s >= LAG[0]) & (s < KVH + LAG[0]))
        def _():
            g = s - LAG[0]
            for d in (1, 2, 3):
                z_in(d, g).wait_recv()
            row_in(1, g).start()
            row_in(0, g).start()
            y_in(2, g).wait_recv()
            k_in(g).start()

        @pl.when((s >= LAG[1]) & (s < KVH + LAG[1]))
        def _():
            g = s - LAG[1]
            k_in(g).wait_recv()
            row_in(1, g).wait_recv()
            row_in(0, g).wait_recv()
            compute(g)
            k_out(g).start()
            row_out(0, g).start()
            row_out(1, g).start()

        @pl.when((s >= LAG[2]) & (s < KVH + LAG[2]))
        def _():
            g = s - LAG[2]
            k_out(g).wait_recv()
            acc[0, g, second] += crossr[g].astype(jnp.float32)
            for n in range(2):
                prev[n, g, 1] = acc[n, g, 2].astype(jnp.bfloat16)
            y_out(1, g).start()
            for n in range(2):
                row_out(n, g).wait_recv()
                rows = slice(1 - n, 3)
                acc[n, g, 4 - n : 6] += partr[n, g, rows].astype(jnp.float32)
                side[n, g] = acc[n, g, 3:6].astype(jnp.bfloat16)
            for d in (2, 1, 3):
                z_out(d, g).start()

        @pl.when((s >= LAG[3]) & (s < KVH + LAG[3]))
        def _():
            g = s - LAG[3]
            y_out(1, g).wait_recv()
            for n in range(2):
                acc[n, g, 1] += prevr[n, g, 1].astype(jnp.float32)
            for d in (1, 2, 3):
                z_out(d, g).wait_recv()
                for n in range(2):
                    acc[n, g, firsts[d - 1]] += sider[d - 1, n, g].astype(jnp.float32)
            for n in range(2):
                prev[n, g, 0] = acc[n, g, 1].astype(jnp.bfloat16)
            y_out(0, g).start()

        @pl.when(s >= LAG[4])
        def _():
            g = s - LAG[4]
            y_out(0, g).wait_recv()
            for n, ref in ((0, gk_ref), (1, gv_ref)):
                total = acc[n, g, 0] + prevr[n, g, 0].astype(jnp.float32)
                ref[:, columns(g, HDIM)] = total.astype(jnp.bfloat16)

        return carry

    lax.fori_loop(0, KVH + LAG[4], step, 0)

    def drain(g, carry):
        k_in(g).wait_send()
        k_out(g).wait_send()
        for n in range(2):
            y_in(n + 1, g).wait_send()
            row_in(n, g).wait_send()
            row_out(n, g).wait_send()
            y_out(n, g).wait_send()
        for d in (1, 2, 3):
            z_in(d, g).wait_send()
            z_out(d, g).wait_send()
        store_wide(g).wait()
        return carry

    lax.fori_loop(0, KVH, drain, 0)


def shards(queries, keys, values, outputs, grad_out, lse_saved, doc_lengths):
    half, full = jnp.bfloat16, jnp.float32
    anywhere = pl.BlockSpec(memory_space=pl.ANY)
    vmem = pl.BlockSpec(memory_space=pltpu.VMEM)
    return pl.pallas_call(
        kernel,
        out_shape=(
            jax.ShapeDtypeStruct((ROWS, HEADS * HDIM), half),
            jax.ShapeDtypeStruct((ROWS, KVH * HDIM), half),
            jax.ShapeDtypeStruct((ROWS, KVH * HDIM), half),
        ),
        in_specs=[anywhere] * 5 + [vmem, pl.BlockSpec(memory_space=pltpu.SMEM)],
        out_specs=(anywhere, vmem, vmem),
        scratch_shapes=[
            pltpu.VMEM((2, KVH, SLOTS, ROWS, HDIM), half),
            pltpu.VMEM((2, KVH, 3, ROWS, HDIM), half),
            pltpu.VMEM((2, KVH, 6, ROWS, HDIM), full),
            pltpu.VMEM((2, KVH, 3, ROWS, HDIM), half),
            pltpu.VMEM((KVH, ROWS, HDIM), half),
            pltpu.VMEM((KVH, ROWS, HDIM), half),
            pltpu.VMEM((2, KVH, 3, ROWS, HDIM), half),
            pltpu.VMEM((3, 2, KVH, ROWS, HDIM), half),
            pltpu.VMEM((2, KVH, 2, ROWS, HDIM), half),
            pltpu.VMEM((2, KVH, 2, ROWS, HDIM), half),
            pltpu.VMEM((KVH, ROWS, WIDE), half),
            pltpu.VMEM((KVH, ROWS, WIDE), half),
            pltpu.VMEM((KVH, ROWS, WIDE), half),
            pltpu.VMEM((KVH, ROWS, WIDE), half),
            pltpu.VMEM((WIDE, HDIM), half),
            pltpu.VMEM((WIDE, HDIM), half),
            pltpu.VMEM((HEADS, ROWS), full),
            pltpu.VMEM((1, WIDE), full),
            pltpu.VMEM((1, WIDE), full),
            pltpu.VMEM((KEYS, ROWS), full),
            pltpu.SemaphoreType.DMA((3, KVH)),
            pltpu.SemaphoreType.DMA((2, KVH)),
            pltpu.SemaphoreType.DMA((KVH,)),
            pltpu.SemaphoreType.DMA((16, KVH)),
            pltpu.SemaphoreType.DMA((16, KVH)),
        ],
        compiler_params=pltpu.CompilerParams(
            collective_id=0,
            has_side_effects=True,
            vmem_limit_bytes=62 * 1024 * 1024,
        ),
        name="attention_backward",
    )(queries, keys, values, outputs, grad_out, lse_saved.T, doc_lengths)


def solution(mesh):
    placed = P(("packs", "seq"), None)
    return jax.shard_map(
        shards,
        mesh=mesh,
        in_specs=(placed,) * 6 + (P("packs"),),
        out_specs=(placed,) * 3,
        check_vma=False,
    )
```

```python
import functools

import jax
import jax.numpy as jnp
from jax import lax
from jax.experimental import pallas as pl
from jax.experimental.pallas import tpu as pltpu
from jax.sharding import PartitionSpec as P

HEADS = 64
KVH = 8
HDIM = 128
GROUP = HEADS // KVH
ROWS = 128
WIDE = GROUP * HDIM
SIDE = 4
SLOTS = 9
KEYS = SLOTS * ROWS
DOCS = 8
LAG = (1, 2, 3, 4, 5)
LOOK = 3
CROSS = ((0, 0), (0, 1))
ROWSPAN = tuple((int((n, 0) in CROSS), 3 - int((n, 1) in CROSS)) for n in range(2))
SCALE = 1.0 / HDIM**0.5
LOG2E = 1.4426950408889634
MESH = pl.DeviceIdType.MESH


def kernel(
    q_hbm,
    k_hbm,
    v_hbm,
    o_hbm,
    go_hbm,
    lse_ref,
    doc_ref,
    gq_hbm,
    gk_ref,
    gv_ref,
    kvw,
    part,
    acc,
    partr,
    crossr,
    side,
    sider,
    prev,
    prevr,
    qb,
    gb,
    ob,
    gqb,
    qs,
    gs,
    lse_t,
    nlse,
    delta,
    bias,
    dq,
    in_sem,
    kv_sem,
    out_sem,
    send_sem,
    recv_sem,
):
    me = lax.axis_index("seq")
    y, z = me // SIDE, lax.rem(me, SIDE)

    def at(dy, dz):
        return lax.rem(y + dy + SIDE, SIDE) * SIDE + lax.rem(z + dz + SIDE, SIDE)

    def remote(src, dst, kind, g, target):
        return pltpu.make_async_remote_copy(
            src_ref=src,
            dst_ref=dst,
            send_sem=send_sem.at[kind, g],
            recv_sem=recv_sem.at[kind, g],
            device_id={"seq": target},
            device_id_type=MESH,
        )

    firsts = (jnp.where(z < 3, 0, 1), jnp.where(z < 2, 0, 1), jnp.where(z < 1, 0, 1))

    def y_in(j, g):
        return remote(kvw.at[:, g, j - 1], kvw.at[:, g, j], j - 1, g, at(1, 0))

    def z_in(d, g):
        return remote(kvw.at[:, g, firsts[d - 1]], kvw.at[:, g, 2 + d], 1 + d, g, at(0, d))

    seconds = (firsts[0] + 1, firsts[2] + 1)

    def cross_in(n, e, g):
        return remote(
            kvw.at[n, g, seconds[e]], kvw.at[n, g, 6 + 2 * e], 5 + 2 * n + e, g, at(0, 1 - 2 * e)
        )

    def cross_out(n, e, g):
        return remote(
            part.at[n, g, 2 * e], crossr.at[n, e, g], 9 + 2 * n + e, g, at(0, 2 * e - 1)
        )

    def row_in(n, g):
        low, high = ROWSPAN[n]
        src, dst = pl.ds(3 + low, high - low), pl.ds(6 + low, high - low)
        return remote(kvw.at[n, g, src], kvw.at[n, g, dst], 13 + n, g, at(1, 0))

    def row_out(n, g):
        low, high = ROWSPAN[n]
        rows = pl.ds(low, high - low)
        return remote(part.at[n, g, rows], partr.at[n, g, rows], 15 + n, g, at(-1, 0))

    def z_out(d, n, g):
        return remote(
            side.at[n, g, d - 1], sider.at[d - 1, n, g], 14 + 3 * n + d + 2, g, at(0, -d)
        )

    def y_out(j, n, g):
        return remote(prev.at[n, g, j], prevr.at[n, g, j], 23 + 2 * j + n, g, at(-1, 0))

    def columns(g, width):
        return pl.ds(pl.multiple_of(g * width, width), width)

    def load_kv(n, g):
        src = (k_hbm, v_hbm)[n]
        return pltpu.make_async_copy(
            src.at[:, columns(g, HDIM)], kvw.at[n, g, 0], kv_sem.at[n, g]
        )

    def load_wide(n, g):
        src, dst = ((q_hbm, qb), (go_hbm, gb), (o_hbm, ob))[n]
        return pltpu.make_async_copy(src.at[:, columns(g, WIDE)], dst.at[g], in_sem.at[n, g])

    def store_wide(g):
        return pltpu.make_async_copy(gqb.at[g], gq_hbm.at[:, columns(g, WIDE)], out_sem.at[g])

    for g in range(KVH):
        load_kv(0, g).start()
        load_kv(1, g).start()
    for g in range(KVH):
        for n in range(3):
            load_wide(n, g).start()

    barrier = pltpu.get_barrier_semaphore()
    for dy, dz in ((1, 0), (2, 0), (3, 0), (0, 1), (0, 2), (0, 3)):
        pl.semaphore_signal(
            barrier, inc=1, device_id={"seq": at(dy, dz)}, device_id_type=MESH
        )
    pl.semaphore_wait(barrier, 6)

    def send_first(g):
        load_kv(0, g).wait()
        load_kv(1, g).wait()
        y_in(1, g).start()

    for g in range(LOOK):
        send_first(g)

    lse_t[...] = lse_ref[...] * LOG2E
    time = lax.broadcasted_iota(jnp.int32, (1, ROWS), 1) + me * ROWS
    begin = jnp.zeros((1, ROWS), jnp.int32)
    bound = doc_ref[0]
    for n in range(1, DOCS):
        begin = jnp.where(time >= bound, bound, begin)
        bound = bound + doc_ref[n]
    for slot in range(SLOTS):
        back = (0, 4, 8, 1, 2, 3, 5, 6, 7)[slot]
        row = lax.rem(me - back + SIDE * SIDE, SIDE * SIDE)
        keys_at = lax.broadcasted_iota(jnp.int32, (ROWS, ROWS), 0) + row * ROWS
        seen = (keys_at <= time) & (keys_at >= begin)
        bias[pl.ds(slot * ROWS, ROWS), :] = jnp.where(seen, 0.0, -1e30)

    def prepare(g):
        for n in range(3):
            load_wide(n, g).wait()
        logs = lse_t[pl.ds(pl.multiple_of(g * GROUP, GROUP), GROUP), :]
        for h in range(GROUP):
            cut = slice(h * HDIM, (h + 1) * HDIM)
            query, gout = qb[g, :, cut], gb[g, :, cut]
            qs[cut, :] = query
            gs[cut, :] = gout
            product = ob[g, :, cut].astype(jnp.float32) * gout.astype(jnp.float32)
            delta[:, cut] = jnp.sum(product.T, axis=0, keepdims=True)
            nlse[:, cut] = logs[h : h + 1, :]

    def attend(g, low, high):
        rows = (high - low) * ROWS
        k = kvw[0, g, low:high].reshape(rows, HDIM)
        v = kvw[1, g, low:high].reshape(rows, HDIM)
        nt = (((1,), (1,)), ((), ()))
        tn = (((0,), (0,)), ((), ()))
        scores = lax.dot_general(k, qs[...], nt, preferred_element_type=jnp.float32)
        hidden = jnp.concatenate([bias[low * ROWS : high * ROWS, :]] * GROUP, axis=1)
        prob = jnp.exp2(scores * (SCALE * LOG2E) - nlse[...] + hidden)
        grad_prob = lax.dot_general(v, gs[...], nt, preferred_element_type=jnp.float32)
        grad_score = (prob * (grad_prob - delta[...])).astype(jnp.bfloat16)
        half = prob.astype(jnp.bfloat16)
        grad_v = jnp.dot(half, gs[...], preferred_element_type=jnp.float32)
        grad_k = jnp.dot(grad_score, qs[...], preferred_element_type=jnp.float32) * SCALE
        grad_q = lax.dot_general(k, grad_score, tn, preferred_element_type=jnp.float32)
        shape = (high - low, ROWS, HDIM)
        return grad_q, grad_k.reshape(shape), grad_v.reshape(shape)

    def near(g):
        prepare(g)
        grad_q, grad_k, grad_v = attend(g, 0, 6)
        dq[...] = grad_q
        acc[0, g] = grad_k
        acc[1, g] = grad_v

    def distant(g):
        grad_q, grad_k, grad_v = attend(g, 6, 9)
        part[0, g] = grad_k.astype(jnp.bfloat16)
        part[1, g] = grad_v.astype(jnp.bfloat16)
        dq[...] += grad_q

    def finish(g):
        for h in range(GROUP):
            cut = slice(h * HDIM, (h + 1) * HDIM)
            gqb[g, :, cut] = (dq[:, cut].T * SCALE).astype(jnp.bfloat16)
        store_wide(g).start()

    def step(s, carry):
        @pl.when(s < KVH)
        def _():
            y_in(1, s).wait_recv()
            for d in (1, 2, 3):
                z_in(d, s).start()
            y_in(2, s).start()

            @pl.when(s < KVH - LOOK)
            def _():
                send_first(s + LOOK)

        @pl.when((s >= LAG[0]) & (s < KVH + LAG[0]))
        def _():
            g = s - LAG[0]
            for d in (1, 2, 3):
                z_in(d, g).wait_recv()
            row_in(0, g).start()
            row_in(1, g).start()
            y_in(2, g).wait_recv()
            for n, e in CROSS:
                cross_in(n, e, g).start()

        @pl.when((s >= LAG[1]) & (s < KVH + LAG[1]))
        def _():
            g = s - LAG[1]
            for n, e in CROSS:
                cross_in(n, e, g).wait_recv()
            row_in(0, g).wait_recv()
            row_in(1, g).wait_recv()
            distant(g)
            for n, e in CROSS:
                cross_out(n, e, g).start()
            row_out(0, g).start()
            row_out(1, g).start()
            finish(g)

        @pl.when((s >= LAG[2]) & (s < KVH + LAG[2]))
        def _():
            g = s - LAG[2]
            for n, e in CROSS:
                cross_out(n, e, g).wait_recv()
                acc[n, g, seconds[e]] += crossr[n, e, g].astype(jnp.float32)
            for n in range(2):
                prev[n, g, 1] = acc[n, g, 2].astype(jnp.bfloat16)
                y_out(1, n, g).start()
            for n in range(2):
                row_out(n, g).wait_recv()
                low, high = ROWSPAN[n]
                acc[n, g, 3 + low : 3 + high] += partr[n, g, low:high].astype(jnp.float32)
                side[n, g] = acc[n, g, 3:6].astype(jnp.bfloat16)
                for d in (2, 1, 3):
                    z_out(d, n, g).start()

        @pl.when((s >= LAG[1] - 1) & (s < KVH + LAG[1] - 1))
        def _():
            near(s - LAG[1] + 1)

        @pl.when((s >= LAG[3]) & (s < KVH + LAG[3]))
        def _():
            g = s - LAG[3]
            for n in range(2):
                y_out(1, n, g).wait_recv()
                acc[n, g, 1] += prevr[n, g, 1].astype(jnp.float32)
                for d in (1, 3, 2):
                    z_out(d, n, g).wait_recv()
                    acc[n, g, firsts[d - 1]] += sider[d - 1, n, g].astype(jnp.float32)
                prev[n, g, 0] = acc[n, g, 1].astype(jnp.bfloat16)
                y_out(0, n, g).start()

        @pl.when(s >= LAG[4])
        def _():
            g = s - LAG[4]
            for n, ref in ((0, gk_ref), (1, gv_ref)):
                y_out(0, n, g).wait_recv()
                total = acc[n, g, 0] + prevr[n, g, 0].astype(jnp.float32)
                ref[:, columns(g, HDIM)] = total.astype(jnp.bfloat16)

        return carry

    lax.fori_loop(0, KVH + LAG[4], step, 0)

    def drain(g, carry):
        for n, e in CROSS:
            cross_in(n, e, g).wait_send()
            cross_out(n, e, g).wait_send()
        for d in (1, 2, 3):
            z_in(d, g).wait_send()
        for n in range(2):
            y_in(n + 1, g).wait_send()
            row_in(n, g).wait_send()
            row_out(n, g).wait_send()
            for j in range(2):
                y_out(j, n, g).wait_send()
            for d in (1, 2, 3):
                z_out(d, n, g).wait_send()
        store_wide(g).wait()
        return carry

    lax.fori_loop(0, KVH, drain, 0)


def publish(gq_in, gk_in, gv_in, gq_out, gk_out, gv_out, wide, slim, in_sem, out_sem):
    loads, stores = [], []
    for n in range(4):
        rows = pl.ds(n * 32, 32)
        loads.append(pltpu.make_async_copy(gq_in.at[rows], wide.at[rows], in_sem.at[n]))
        stores.append(pltpu.make_async_copy(wide.at[rows], gq_out.at[rows], out_sem.at[n]))
    for n, (src, dst) in enumerate(((gk_in, gk_out), (gv_in, gv_out))):
        loads.append(pltpu.make_async_copy(src, slim.at[n], in_sem.at[4 + n]))
        stores.append(pltpu.make_async_copy(slim.at[n], dst, out_sem.at[4 + n]))
    for load in loads:
        load.start()
    for load, store in zip(loads, stores):
        load.wait()
        store.start()
    for store in stores:
        store.wait()


def shards(queries, keys, values, outputs, grad_out, lse_saved, doc_lengths):
    half, full = jnp.bfloat16, jnp.float32
    anywhere = pl.BlockSpec(memory_space=pl.ANY)
    vmem = pl.BlockSpec(memory_space=pltpu.VMEM)
    grads = pl.pallas_call(
        kernel,
        out_shape=(
            jax.ShapeDtypeStruct((ROWS, HEADS * HDIM), half),
            jax.ShapeDtypeStruct((ROWS, KVH * HDIM), half),
            jax.ShapeDtypeStruct((ROWS, KVH * HDIM), half),
        ),
        in_specs=[anywhere] * 5 + [vmem, pl.BlockSpec(memory_space=pltpu.SMEM)],
        out_specs=(anywhere, vmem, vmem),
        scratch_shapes=[
            pltpu.VMEM((2, KVH, SLOTS, ROWS, HDIM), half),
            pltpu.VMEM((2, KVH, 3, ROWS, HDIM), half),
            pltpu.VMEM((2, KVH, 6, ROWS, HDIM), full),
            pltpu.VMEM((2, KVH, 3, ROWS, HDIM), half),
            pltpu.VMEM((2, 2, KVH, ROWS, HDIM), half),
            pltpu.VMEM((2, KVH, 3, ROWS, HDIM), half),
            pltpu.VMEM((3, 2, KVH, ROWS, HDIM), half),
            pltpu.VMEM((2, KVH, 2, ROWS, HDIM), half),
            pltpu.VMEM((2, KVH, 2, ROWS, HDIM), half),
            pltpu.VMEM((KVH, ROWS, WIDE), half),
            pltpu.VMEM((KVH, ROWS, WIDE), half),
            pltpu.VMEM((KVH, ROWS, WIDE), half),
            pltpu.VMEM((KVH, ROWS, WIDE), half),
            pltpu.VMEM((WIDE, HDIM), half),
            pltpu.VMEM((WIDE, HDIM), half),
            pltpu.VMEM((HEADS, ROWS), full),
            pltpu.VMEM((1, WIDE), full),
            pltpu.VMEM((1, WIDE), full),
            pltpu.VMEM((KEYS, ROWS), full),
            pltpu.VMEM((HDIM, WIDE), full),
            pltpu.SemaphoreType.DMA((3, KVH)),
            pltpu.SemaphoreType.DMA((2, KVH)),
            pltpu.SemaphoreType.DMA((KVH,)),
            pltpu.SemaphoreType.DMA((27, KVH)),
            pltpu.SemaphoreType.DMA((27, KVH)),
        ],
        compiler_params=pltpu.CompilerParams(
            collective_id=0,
            has_side_effects=True,
            vmem_limit_bytes=62 * 1024 * 1024,
        ),
        name="attention_backward",
    )(queries, keys, values, outputs, grad_out, lse_saved.T, doc_lengths)
    return pl.pallas_call(
        publish,
        out_shape=(
            jax.ShapeDtypeStruct((ROWS, HEADS * HDIM), half),
            jax.ShapeDtypeStruct((ROWS, KVH * HDIM), half),
            jax.ShapeDtypeStruct((ROWS, KVH * HDIM), half),
        ),
        in_specs=[anywhere] * 3,
        out_specs=(anywhere,) * 3,
        scratch_shapes=[
            pltpu.VMEM((ROWS, HEADS * HDIM), half),
            pltpu.VMEM((2, ROWS, KVH * HDIM), half),
            pltpu.SemaphoreType.DMA((6,)),
            pltpu.SemaphoreType.DMA((6,)),
        ],
        name="publish",
    )(*grads)


def solution(mesh):
    placed = P(("packs", "seq"), None)
    return jax.shard_map(
        shards,
        mesh=mesh,
        in_specs=(placed,) * 6 + (P("packs"),),
        out_specs=(placed,) * 3,
        check_vma=False,
    )
```

```python
import functools

import jax
import jax.numpy as jnp
from jax import lax
from jax.experimental import pallas as pl
from jax.experimental.pallas import tpu as pltpu
from jax.sharding import PartitionSpec as P

HEADS = 64
KVH = 8
HDIM = 128
GROUP = HEADS // KVH
ROWS = 128
WIDE = GROUP * HDIM
SIDE = 4
SLOTS = 9
KEYS = SLOTS * ROWS
DOCS = 8
LAG = (1, 2, 3, 4, 5)
LOOK = 3
HEAVY = ((0, 0), (0, 1), (1, 0), (1, 1))
LIGHT = ((0, 0),)
LEAD = 2
TAIL = 2
SCALE = 1.0 / HDIM**0.5
LOG2E = 1.4426950408889634
MESH = pl.DeviceIdType.MESH


def kernel(
    q_hbm,
    k_hbm,
    v_hbm,
    o_hbm,
    go_hbm,
    lse_ref,
    doc_ref,
    gq_hbm,
    gk_hbm,
    gv_hbm,
    kvw,
    part,
    acc,
    partr,
    crossr,
    side,
    sider,
    prev,
    prevr,
    qb,
    gb,
    ob,
    gqb,
    qs,
    gs,
    lse_t,
    nlse,
    delta,
    bias,
    dq,
    slim,
    in_sem,
    kv_sem,
    out_sem,
    slim_sem,
    send_sem,
    recv_sem,
):
    me = lax.axis_index("seq")
    y, z = me // SIDE, lax.rem(me, SIDE)

    def at(dy, dz):
        return lax.rem(y + dy + SIDE, SIDE) * SIDE + lax.rem(z + dz + SIDE, SIDE)

    def remote(src, dst, kind, g, target):
        return pltpu.make_async_remote_copy(
            src_ref=src,
            dst_ref=dst,
            send_sem=send_sem.at[kind, g],
            recv_sem=recv_sem.at[kind, g],
            device_id={"seq": target},
            device_id_type=MESH,
        )

    firsts = (jnp.where(z < 3, 0, 1), jnp.where(z < 2, 0, 1), jnp.where(z < 1, 0, 1))

    def y_in(j, g):
        return remote(kvw.at[:, g, j - 1], kvw.at[:, g, j], j - 1, g, at(1, 0))

    def z_in(d, g):
        return remote(kvw.at[:, g, firsts[d - 1]], kvw.at[:, g, 2 + d], 1 + d, g, at(0, d))

    seconds = (firsts[0] + 1, firsts[2] + 1)

    def cross_in(n, e, g):
        return remote(
            kvw.at[n, g, seconds[e]], kvw.at[n, g, 6 + 2 * e], 5 + 2 * n + e, g, at(0, 1 - 2 * e)
        )

    def cross_out(n, e, g):
        return remote(
            part.at[n, g, 2 * e], crossr.at[n, e, g], 9 + 2 * n + e, g, at(0, 2 * e - 1)
        )

    def span(n, cross):
        return int((n, 0) in cross), 3 - int((n, 1) in cross)

    def row_in(n, cross, g):
        low, high = span(n, cross)
        src, dst = pl.ds(3 + low, high - low), pl.ds(6 + low, high - low)
        return remote(kvw.at[n, g, src], kvw.at[n, g, dst], 13 + n, g, at(1, 0))

    def row_out(n, cross, g):
        low, high = span(n, cross)
        rows = pl.ds(low, high - low)
        return remote(part.at[n, g, rows], partr.at[n, g, rows], 15 + n, g, at(-1, 0))

    def by_load(heavy, body):
        @pl.when(heavy)
        def _():
            body(HEAVY)

        @pl.when(jnp.logical_not(heavy))
        def _():
            body(LIGHT)

    def in_load(g, body):
        by_load(g < LEAD, body)

    def out_load(g, body):
        by_load(g >= KVH - TAIL, body)

    def z_out(d, n, g):
        return remote(
            side.at[n, g, d - 1], sider.at[d - 1, n, g], 14 + 3 * n + d + 2, g, at(0, -d)
        )

    def y_out(j, n, g):
        return remote(prev.at[n, g, j], prevr.at[n, g, j], 23 + 2 * j + n, g, at(-1, 0))

    def columns(g, width):
        return pl.ds(pl.multiple_of(g * width, width), width)

    def load_kv(n, g):
        src = (k_hbm, v_hbm)[n]
        return pltpu.make_async_copy(
            src.at[:, columns(g, HDIM)], kvw.at[n, g, 0], kv_sem.at[n, g]
        )

    def load_wide(n, g):
        src, dst = ((q_hbm, qb), (go_hbm, gb), (o_hbm, ob))[n]
        return pltpu.make_async_copy(src.at[:, columns(g, WIDE)], dst.at[g], in_sem.at[n, g])

    def store_slim(n, g):
        dst = (gk_hbm, gv_hbm)[n]
        return pltpu.make_async_copy(slim.at[n, g], dst.at[:, columns(g, HDIM)], slim_sem.at[n, g])

    def store_wide(g):
        return pltpu.make_async_copy(gqb.at[g], gq_hbm.at[:, columns(g, WIDE)], out_sem.at[g])

    for g in range(KVH):
        load_kv(0, g).start()
        load_kv(1, g).start()
    for g in range(KVH):
        for n in range(3):
            load_wide(n, g).start()

    barrier = pltpu.get_barrier_semaphore()
    for dy, dz in ((1, 0), (2, 0), (3, 0), (0, 1), (0, 2), (0, 3)):
        pl.semaphore_signal(
            barrier, inc=1, device_id={"seq": at(dy, dz)}, device_id_type=MESH
        )
    pl.semaphore_wait(barrier, 6)

    def send_first(g):
        load_kv(0, g).wait()
        load_kv(1, g).wait()
        y_in(1, g).start()

    for g in range(LOOK):
        send_first(g)

    lse_t[...] = lse_ref[...] * LOG2E
    time = lax.broadcasted_iota(jnp.int32, (1, ROWS), 1) + me * ROWS
    begin = jnp.zeros((1, ROWS), jnp.int32)
    bound = doc_ref[0]
    for n in range(1, DOCS):
        begin = jnp.where(time >= bound, bound, begin)
        bound = bound + doc_ref[n]
    for slot in range(SLOTS):
        back = (0, 4, 8, 1, 2, 3, 5, 6, 7)[slot]
        row = lax.rem(me - back + SIDE * SIDE, SIDE * SIDE)
        keys_at = lax.broadcasted_iota(jnp.int32, (ROWS, ROWS), 0) + row * ROWS
        seen = (keys_at <= time) & (keys_at >= begin)
        bias[pl.ds(slot * ROWS, ROWS), :] = jnp.where(seen, 0.0, -1e30)

    def prepare(g):
        for n in range(3):
            load_wide(n, g).wait()
        logs = lse_t[pl.ds(pl.multiple_of(g * GROUP, GROUP), GROUP), :]
        for h in range(GROUP):
            cut = slice(h * HDIM, (h + 1) * HDIM)
            query, gout = qb[g, :, cut], gb[g, :, cut]
            qs[cut, :] = query
            gs[cut, :] = gout
            product = ob[g, :, cut].astype(jnp.float32) * gout.astype(jnp.float32)
            delta[:, cut] = jnp.sum(product.T, axis=0, keepdims=True)
            nlse[:, cut] = logs[h : h + 1, :]

    def attend(g, low, high):
        rows = (high - low) * ROWS
        k = kvw[0, g, low:high].reshape(rows, HDIM)
        v = kvw[1, g, low:high].reshape(rows, HDIM)
        nt = (((1,), (1,)), ((), ()))
        tn = (((0,), (0,)), ((), ()))
        scores = lax.dot_general(k, qs[...], nt, preferred_element_type=jnp.float32)
        hidden = jnp.concatenate([bias[low * ROWS : high * ROWS, :]] * GROUP, axis=1)
        prob = jnp.exp2(scores * (SCALE * LOG2E) - nlse[...] + hidden)
        grad_prob = lax.dot_general(v, gs[...], nt, preferred_element_type=jnp.float32)
        grad_score = (prob * (grad_prob - delta[...])).astype(jnp.bfloat16)
        half = prob.astype(jnp.bfloat16)
        grad_v = jnp.dot(half, gs[...], preferred_element_type=jnp.float32)
        grad_k = jnp.dot(grad_score, qs[...], preferred_element_type=jnp.float32) * SCALE
        grad_q = lax.dot_general(k, grad_score, tn, preferred_element_type=jnp.float32)
        shape = (high - low, ROWS, HDIM)
        return grad_q, grad_k.reshape(shape), grad_v.reshape(shape)

    def near(g):
        prepare(g)
        grad_q, grad_k, grad_v = attend(g, 0, 6)
        dq[...] = grad_q
        acc[0, g] = grad_k
        acc[1, g] = grad_v

    def distant(g):
        grad_q, grad_k, grad_v = attend(g, 6, 9)
        part[0, g] = grad_k.astype(jnp.bfloat16)
        part[1, g] = grad_v.astype(jnp.bfloat16)
        dq[...] += grad_q

    def finish(g):
        for h in range(GROUP):
            cut = slice(h * HDIM, (h + 1) * HDIM)
            gqb[g, :, cut] = (dq[:, cut].T * SCALE).astype(jnp.bfloat16)
        store_wide(g).start()

    def step(s, carry):
        @pl.when(s < KVH)
        def _():
            y_in(1, s).wait_recv()
            for d in (1, 2, 3):
                z_in(d, s).start()
            y_in(2, s).start()

            @pl.when(s < KVH - LOOK)
            def _():
                send_first(s + LOOK)

        @pl.when((s >= LAG[0]) & (s < KVH + LAG[0]))
        def _():
            g = s - LAG[0]
            for d in (1, 2, 3):
                z_in(d, g).wait_recv()

            def send(cross):
                row_in(0, cross, g).start()
                row_in(1, cross, g).start()
                y_in(2, g).wait_recv()
                for n, e in cross:
                    cross_in(n, e, g).start()

            in_load(g, send)

        @pl.when((s >= LAG[1]) & (s < KVH + LAG[1]))
        def _():
            g = s - LAG[1]

            def arrive(cross):
                for n, e in cross:
                    cross_in(n, e, g).wait_recv()
                for n in range(2):
                    row_in(n, cross, g).wait_recv()

            def leave(cross):
                for n, e in cross:
                    cross_out(n, e, g).start()
                for n in range(2):
                    row_out(n, cross, g).start()

            in_load(g, arrive)
            distant(g)
            out_load(g, leave)
            finish(g)

        @pl.when((s >= LAG[2]) & (s < KVH + LAG[2]))
        def _():
            g = s - LAG[2]

            def collect(cross):
                for n, e in cross:
                    cross_out(n, e, g).wait_recv()
                    acc[n, g, seconds[e]] += crossr[n, e, g].astype(jnp.float32)
                for n in range(2):
                    prev[n, g, 1] = acc[n, g, 2].astype(jnp.bfloat16)
                    y_out(1, n, g).start()
                for n in range(2):
                    row_out(n, cross, g).wait_recv()
                    low, high = span(n, cross)
                    acc[n, g, 3 + low : 3 + high] += partr[n, g, low:high].astype(jnp.float32)
                    side[n, g] = acc[n, g, 3:6].astype(jnp.bfloat16)
                    for d in (2, 1, 3):
                        z_out(d, n, g).start()

            out_load(g, collect)

        @pl.when((s >= LAG[1] - 1) & (s < KVH + LAG[1] - 1))
        def _():
            near(s - LAG[1] + 1)

        @pl.when((s >= LAG[3]) & (s < KVH + LAG[3]))
        def _():
            g = s - LAG[3]
            for n in range(2):
                y_out(1, n, g).wait_recv()
                acc[n, g, 1] += prevr[n, g, 1].astype(jnp.float32)
                for d in (1, 3, 2):
                    z_out(d, n, g).wait_recv()
                    acc[n, g, firsts[d - 1]] += sider[d - 1, n, g].astype(jnp.float32)
                prev[n, g, 0] = acc[n, g, 1].astype(jnp.bfloat16)
                y_out(0, n, g).start()

        @pl.when(s >= LAG[4])
        def _():
            g = s - LAG[4]
            for n in range(2):
                y_out(0, n, g).wait_recv()
                total = acc[n, g, 0] + prevr[n, g, 0].astype(jnp.float32)
                slim[n, g] = total.astype(jnp.bfloat16)
                store_slim(n, g).start()

        return carry

    lax.fori_loop(0, KVH + LAG[4], step, 0)

    def drain(g, carry):
        def sent_in(cross):
            for n, e in cross:
                cross_in(n, e, g).wait_send()
            for n in range(2):
                row_in(n, cross, g).wait_send()

        def sent_out(cross):
            for n, e in cross:
                cross_out(n, e, g).wait_send()
            for n in range(2):
                row_out(n, cross, g).wait_send()

        in_load(g, sent_in)
        out_load(g, sent_out)
        for d in (1, 2, 3):
            z_in(d, g).wait_send()
        for n in range(2):
            y_in(n + 1, g).wait_send()
            for j in range(2):
                y_out(j, n, g).wait_send()
            for d in (1, 2, 3):
                z_out(d, n, g).wait_send()
        store_wide(g).wait()
        store_slim(0, g).wait()
        store_slim(1, g).wait()
        return carry

    lax.fori_loop(0, KVH, drain, 0)


def publish(gq_in, gk_in, gv_in, gq_out, gk_out, gv_out, wide, slim, in_sem, out_sem):
    loads, stores = [], []
    for n in range(8):
        rows = pl.ds(n * 16, 16)
        loads.append(pltpu.make_async_copy(gq_in.at[rows], wide.at[rows], in_sem.at[n]))
        stores.append(pltpu.make_async_copy(wide.at[rows], gq_out.at[rows], out_sem.at[n]))
    for n, (src, dst) in enumerate(((gk_in, gk_out), (gv_in, gv_out))):
        loads.append(pltpu.make_async_copy(src, slim.at[n], in_sem.at[8 + n]))
        stores.append(pltpu.make_async_copy(slim.at[n], dst, out_sem.at[8 + n]))
    for load in loads:
        load.start()
    for load, store in zip(loads, stores):
        load.wait()
        store.start()
    for store in stores:
        store.wait()


def shards(queries, keys, values, outputs, grad_out, lse_saved, doc_lengths):
    half, full = jnp.bfloat16, jnp.float32
    anywhere = pl.BlockSpec(memory_space=pl.ANY)
    vmem = pl.BlockSpec(memory_space=pltpu.VMEM)
    grads = pl.pallas_call(
        kernel,
        out_shape=(
            jax.ShapeDtypeStruct((ROWS, HEADS * HDIM), half),
            jax.ShapeDtypeStruct((ROWS, KVH * HDIM), half),
            jax.ShapeDtypeStruct((ROWS, KVH * HDIM), half),
        ),
        in_specs=[anywhere] * 5 + [vmem, pl.BlockSpec(memory_space=pltpu.SMEM)],
        out_specs=(anywhere,) * 3,
        scratch_shapes=[
            pltpu.VMEM((2, KVH, SLOTS, ROWS, HDIM), half),
            pltpu.VMEM((2, KVH, 3, ROWS, HDIM), half),
            pltpu.VMEM((2, KVH, 6, ROWS, HDIM), full),
            pltpu.VMEM((2, KVH, 3, ROWS, HDIM), half),
            pltpu.VMEM((2, 2, KVH, ROWS, HDIM), half),
            pltpu.VMEM((2, KVH, 3, ROWS, HDIM), half),
            pltpu.VMEM((3, 2, KVH, ROWS, HDIM), half),
            pltpu.VMEM((2, KVH, 2, ROWS, HDIM), half),
            pltpu.VMEM((2, KVH, 2, ROWS, HDIM), half),
            pltpu.VMEM((KVH, ROWS, WIDE), half),
            pltpu.VMEM((KVH, ROWS, WIDE), half),
            pltpu.VMEM((KVH, ROWS, WIDE), half),
            pltpu.VMEM((KVH, ROWS, WIDE), half),
            pltpu.VMEM((WIDE, HDIM), half),
            pltpu.VMEM((WIDE, HDIM), half),
            pltpu.VMEM((HEADS, ROWS), full),
            pltpu.VMEM((1, WIDE), full),
            pltpu.VMEM((1, WIDE), full),
            pltpu.VMEM((KEYS, ROWS), full),
            pltpu.VMEM((HDIM, WIDE), full),
            pltpu.VMEM((2, KVH, ROWS, HDIM), half),
            pltpu.SemaphoreType.DMA((3, KVH)),
            pltpu.SemaphoreType.DMA((2, KVH)),
            pltpu.SemaphoreType.DMA((KVH,)),
            pltpu.SemaphoreType.DMA((2, KVH)),
            pltpu.SemaphoreType.DMA((27, KVH)),
            pltpu.SemaphoreType.DMA((27, KVH)),
        ],
        compiler_params=pltpu.CompilerParams(
            collective_id=0,
            has_side_effects=True,
            vmem_limit_bytes=62 * 1024 * 1024,
        ),
        name="attention_backward",
    )(queries, keys, values, outputs, grad_out, lse_saved.T, doc_lengths)
    return pl.pallas_call(
        publish,
        out_shape=(
            jax.ShapeDtypeStruct((ROWS, HEADS * HDIM), half),
            jax.ShapeDtypeStruct((ROWS, KVH * HDIM), half),
            jax.ShapeDtypeStruct((ROWS, KVH * HDIM), half),
        ),
        in_specs=[anywhere] * 3,
        out_specs=(anywhere,) * 3,
        scratch_shapes=[
            pltpu.VMEM((ROWS, HEADS * HDIM), half),
            pltpu.VMEM((2, ROWS, KVH * HDIM), half),
            pltpu.SemaphoreType.DMA((10,)),
            pltpu.SemaphoreType.DMA((10,)),
        ],
        name="publish",
    )(*grads)


def solution(mesh):
    placed = P(("packs", "seq"), None)
    return jax.shard_map(
        shards,
        mesh=mesh,
        in_specs=(placed,) * 6 + (P("packs"),),
        out_specs=(placed,) * 3,
        check_vma=False,
    )
```

```python
import functools

import jax
import jax.numpy as jnp
from jax import lax
from jax.experimental import pallas as pl
from jax.experimental.pallas import tpu as pltpu
from jax.sharding import PartitionSpec as P

HEADS = 64
KVH = 8
HDIM = 128
GROUP = HEADS // KVH
ROWS = 128
WIDE = GROUP * HDIM
SIDE = 4
SLOTS = 9
KEYS = SLOTS * ROWS
DOCS = 8
LAG = (1, 2, 3, 4, 5)
LOOK = 3
HEAVY = ((0, 0), (0, 1), (1, 0), (1, 1))
LIGHT = ((0, 0),)
LEAD = 2
TAIL = 2
SCALE = 1.0 / HDIM**0.5
LOG2E = 1.4426950408889634
MESH = pl.DeviceIdType.MESH


def kernel(
    q_hbm,
    k_hbm,
    v_hbm,
    o_hbm,
    go_hbm,
    lse_ref,
    doc_ref,
    gq_hbm,
    gk_hbm,
    gv_hbm,
    kvw,
    part,
    acc,
    partr,
    crossr,
    side,
    sider,
    prev,
    prevr,
    qb,
    gb,
    ob,
    gqb,
    qs,
    gs,
    lse_t,
    nlse,
    delta,
    bias,
    dq,
    slim,
    in_sem,
    kv_sem,
    out_sem,
    slim_sem,
    send_sem,
    recv_sem,
):
    me = lax.axis_index("seq")
    y, z = me // SIDE, lax.rem(me, SIDE)

    def at(dy, dz):
        return lax.rem(y + dy + SIDE, SIDE) * SIDE + lax.rem(z + dz + SIDE, SIDE)

    def remote(src, dst, kind, g, target):
        return pltpu.make_async_remote_copy(
            src_ref=src,
            dst_ref=dst,
            send_sem=send_sem.at[kind, g],
            recv_sem=recv_sem.at[kind, g],
            device_id={"seq": target},
            device_id_type=MESH,
        )

    firsts = (jnp.where(z < 3, 0, 1), jnp.where(z < 2, 0, 1), jnp.where(z < 1, 0, 1))

    def y_in(j, g):
        return remote(kvw.at[:, g, j - 1], kvw.at[:, g, j], j - 1, g, at(1, 0))

    def z_in(d, g):
        return remote(kvw.at[:, g, firsts[d - 1]], kvw.at[:, g, 2 + d], 1 + d, g, at(0, d))

    seconds = (firsts[0] + 1, firsts[2] + 1)

    def cross_in(n, e, g):
        return remote(
            kvw.at[n, g, seconds[e]], kvw.at[n, g, 6 + 2 * e], 5 + 2 * n + e, g, at(0, 1 - 2 * e)
        )

    def cross_out(n, e, g):
        return remote(
            part.at[n, g, 2 * e], crossr.at[n, e, g], 9 + 2 * n + e, g, at(0, 2 * e - 1)
        )

    def span(n, cross):
        return int((n, 0) in cross), 3 - int((n, 1) in cross)

    def row_in(n, cross, g):
        low, high = span(n, cross)
        src, dst = pl.ds(3 + low, high - low), pl.ds(6 + low, high - low)
        return remote(kvw.at[n, g, src], kvw.at[n, g, dst], 13 + n, g, at(1, 0))

    def row_out(n, cross, g):
        low, high = span(n, cross)
        rows = pl.ds(low, high - low)
        return remote(part.at[n, g, rows], partr.at[n, g, rows], 15 + n, g, at(-1, 0))

    def by_load(heavy, body):
        @pl.when(heavy)
        def _():
            body(HEAVY)

        @pl.when(jnp.logical_not(heavy))
        def _():
            body(LIGHT)

    def in_load(g, body):
        by_load(g < LEAD, body)

    def out_load(g, body):
        by_load(g >= KVH - TAIL, body)

    def z_out(d, n, g):
        return remote(
            side.at[n, g, d - 1], sider.at[d - 1, n, g], 14 + 3 * n + d + 2, g, at(0, -d)
        )

    def y_out(j, n, g):
        return remote(prev.at[n, g, j], prevr.at[n, g, j], 23 + 2 * j + n, g, at(-1, 0))

    def columns(g, width):
        return pl.ds(pl.multiple_of(g * width, width), width)

    def load_kv(n, g):
        src = (k_hbm, v_hbm)[n]
        return pltpu.make_async_copy(
            src.at[:, columns(g, HDIM)], kvw.at[n, g, 0], kv_sem.at[n, g]
        )

    def load_wide(n, g):
        src, dst = ((q_hbm, qb), (go_hbm, gb), (o_hbm, ob))[n]
        return pltpu.make_async_copy(src.at[:, columns(g, WIDE)], dst.at[g], in_sem.at[n, g])

    def store_slim(n, g):
        dst = (gk_hbm, gv_hbm)[n]
        return pltpu.make_async_copy(slim.at[n, g], dst.at[:, columns(g, HDIM)], slim_sem.at[n, g])

    def store_wide(g):
        return pltpu.make_async_copy(gqb.at[g], gq_hbm.at[:, columns(g, WIDE)], out_sem.at[g])

    for g in range(KVH):
        load_kv(0, g).start()
        load_kv(1, g).start()
    for g in range(KVH):
        for n in range(3):
            load_wide(n, g).start()

    barrier = pltpu.get_barrier_semaphore()
    for dy, dz in ((1, 0), (2, 0), (3, 0), (0, 1), (0, 2), (0, 3)):
        pl.semaphore_signal(
            barrier, inc=1, device_id={"seq": at(dy, dz)}, device_id_type=MESH
        )
    pl.semaphore_wait(barrier, 6)

    def send_first(g):
        load_kv(0, g).wait()
        load_kv(1, g).wait()
        y_in(1, g).start()

    for g in range(LOOK):
        send_first(g)

    lse_t[...] = lse_ref[...] * LOG2E
    time = lax.broadcasted_iota(jnp.int32, (1, ROWS), 1) + me * ROWS
    begin = jnp.zeros((1, ROWS), jnp.int32)
    bound = doc_ref[0]
    for n in range(1, DOCS):
        begin = jnp.where(time >= bound, bound, begin)
        bound = bound + doc_ref[n]
    for slot in range(SLOTS):
        back = (0, 4, 8, 1, 2, 3, 5, 6, 7)[slot]
        row = lax.rem(me - back + SIDE * SIDE, SIDE * SIDE)
        keys_at = lax.broadcasted_iota(jnp.int32, (ROWS, ROWS), 0) + row * ROWS
        seen = (keys_at <= time) & (keys_at >= begin)
        bias[pl.ds(slot * ROWS, ROWS), :] = jnp.where(seen, 0.0, -1e30)

    def prepare(g):
        for n in range(3):
            load_wide(n, g).wait()
        logs = lse_t[pl.ds(pl.multiple_of(g * GROUP, GROUP), GROUP), :]
        for h in range(GROUP):
            cut = slice(h * HDIM, (h + 1) * HDIM)
            query, gout = qb[g, :, cut], gb[g, :, cut]
            qs[cut, :] = query
            gs[cut, :] = gout
            product = ob[g, :, cut].astype(jnp.float32) * gout.astype(jnp.float32)
            delta[:, cut] = jnp.sum(product.T, axis=0, keepdims=True)
            nlse[:, cut] = logs[h : h + 1, :]

    def attend(g, low, high):
        rows = (high - low) * ROWS
        k = kvw[0, g, low:high].reshape(rows, HDIM)
        v = kvw[1, g, low:high].reshape(rows, HDIM)
        nt = (((1,), (1,)), ((), ()))
        tn = (((0,), (0,)), ((), ()))
        scores = lax.dot_general(k, qs[...], nt, preferred_element_type=jnp.float32)
        hidden = jnp.concatenate([bias[low * ROWS : high * ROWS, :]] * GROUP, axis=1)
        prob = jnp.exp2(scores * (SCALE * LOG2E) - nlse[...] + hidden)
        grad_prob = lax.dot_general(v, gs[...], nt, preferred_element_type=jnp.float32)
        grad_score = (prob * (grad_prob - delta[...])).astype(jnp.bfloat16)
        half = prob.astype(jnp.bfloat16)
        grad_v = jnp.dot(half, gs[...], preferred_element_type=jnp.float32)
        grad_k = jnp.dot(grad_score, qs[...], preferred_element_type=jnp.float32) * SCALE
        grad_q = lax.dot_general(k, grad_score, tn, preferred_element_type=jnp.float32)
        shape = (high - low, ROWS, HDIM)
        return grad_q, grad_k.reshape(shape), grad_v.reshape(shape)

    def near(g):
        @pl.when(g > 0)
        def _():
            prepare(g)

        grad_q, grad_k, grad_v = attend(g, 0, 6)
        dq[...] = grad_q
        acc[0, g] = grad_k
        acc[1, g] = grad_v

    def distant(g, leave):
        rows = 3 * ROWS
        k = kvw[0, g, 6:9].reshape(rows, HDIM)
        v = kvw[1, g, 6:9].reshape(rows, HDIM)
        nt = (((1,), (1,)), ((), ()))
        tn = (((0,), (0,)), ((), ()))
        shape = (3, ROWS, HDIM)
        scores = lax.dot_general(k, qs[...], nt, preferred_element_type=jnp.float32)
        hidden = jnp.concatenate([bias[6 * ROWS :, :]] * GROUP, axis=1)
        prob = jnp.exp2(scores * (SCALE * LOG2E) - nlse[...] + hidden)
        half = prob.astype(jnp.bfloat16)
        grad_v = jnp.dot(half, gs[...], preferred_element_type=jnp.float32)
        part[1, g] = grad_v.reshape(shape).astype(jnp.bfloat16)
        leave(1)
        grad_prob = lax.dot_general(v, gs[...], nt, preferred_element_type=jnp.float32)
        grad_score = (prob * (grad_prob - delta[...])).astype(jnp.bfloat16)
        grad_k = jnp.dot(grad_score, qs[...], preferred_element_type=jnp.float32) * SCALE
        part[0, g] = grad_k.reshape(shape).astype(jnp.bfloat16)
        leave(0)
        dq[...] += lax.dot_general(k, grad_score, tn, preferred_element_type=jnp.float32)

    def finish(g):
        for h in range(GROUP):
            cut = slice(h * HDIM, (h + 1) * HDIM)
            gqb[g, :, cut] = (dq[:, cut].T * SCALE).astype(jnp.bfloat16)
        store_wide(g).start()

    def step(s, carry):
        @pl.when(s < KVH)
        def _():
            y_in(1, s).wait_recv()
            for d in (1, 2, 3):
                z_in(d, s).start()
            y_in(2, s).start()

            @pl.when(s < KVH - LOOK)
            def _():
                send_first(s + LOOK)

        @pl.when((s >= LAG[0]) & (s < KVH + LAG[0]))
        def _():
            g = s - LAG[0]
            for d in (1, 2, 3):
                z_in(d, g).wait_recv()

            def send(cross):
                row_in(0, cross, g).start()
                row_in(1, cross, g).start()
                y_in(2, g).wait_recv()
                for n, e in cross:
                    cross_in(n, e, g).start()

            in_load(g, send)

        @pl.when((s >= LAG[1]) & (s < KVH + LAG[1]))
        def _():
            g = s - LAG[1]

            def arrive(cross):
                for n, e in cross:
                    cross_in(n, e, g).wait_recv()
                for n in range(2):
                    row_in(n, cross, g).wait_recv()

            def leave(n):
                def send(cross):
                    for m, e in cross:
                        if m == n:
                            cross_out(n, e, g).start()
                    row_out(n, cross, g).start()

                out_load(g, send)

            in_load(g, arrive)
            distant(g, leave)

        @pl.when((s >= LAG[2]) & (s < KVH + LAG[2]))
        def _():
            g = s - LAG[2]

            def collect(cross):
                for n in (1, 0):
                    for m, e in cross:
                        if m == n:
                            cross_out(n, e, g).wait_recv()
                            acc[n, g, seconds[e]] += crossr[n, e, g].astype(jnp.float32)
                    prev[n, g, 1] = acc[n, g, 2].astype(jnp.bfloat16)
                    y_out(1, n, g).start()
                    row_out(n, cross, g).wait_recv()
                    low, high = span(n, cross)
                    acc[n, g, 3 + low : 3 + high] += partr[n, g, low:high].astype(jnp.float32)
                    side[n, g] = acc[n, g, 3:6].astype(jnp.bfloat16)
                    for d in (2, 1, 3):
                        z_out(d, n, g).start()

            out_load(g, collect)

        @pl.when((s >= LAG[1]) & (s < KVH + LAG[1]))
        def _():
            finish(s - LAG[1])

        @pl.when((s >= LAG[1] - 1) & (s < KVH + LAG[1] - 1))
        def _():
            near(s - LAG[1] + 1)

        @pl.when((s >= LAG[3]) & (s < KVH + LAG[3]))
        def _():
            g = s - LAG[3]
            for n in (1, 0):
                y_out(1, n, g).wait_recv()
                acc[n, g, 1] += prevr[n, g, 1].astype(jnp.float32)
                for d in (1, 3, 2):
                    z_out(d, n, g).wait_recv()
                    acc[n, g, firsts[d - 1]] += sider[d - 1, n, g].astype(jnp.float32)
                prev[n, g, 0] = acc[n, g, 1].astype(jnp.bfloat16)
                y_out(0, n, g).start()

        @pl.when(s >= LAG[4])
        def _():
            g = s - LAG[4]
            for n in range(2):
                y_out(0, n, g).wait_recv()
                total = acc[n, g, 0] + prevr[n, g, 0].astype(jnp.float32)
                slim[n, g] = total.astype(jnp.bfloat16)
                store_slim(n, g).start()

        return carry

    prepare(0)
    lax.fori_loop(0, KVH + LAG[4], step, 0)

    def drain(g, carry):
        def sent_in(cross):
            for n, e in cross:
                cross_in(n, e, g).wait_send()
            for n in range(2):
                row_in(n, cross, g).wait_send()

        def sent_out(cross):
            for n, e in cross:
                cross_out(n, e, g).wait_send()
            for n in range(2):
                row_out(n, cross, g).wait_send()

        in_load(g, sent_in)
        out_load(g, sent_out)
        for d in (1, 2, 3):
            z_in(d, g).wait_send()
        for n in range(2):
            y_in(n + 1, g).wait_send()
            for j in range(2):
                y_out(j, n, g).wait_send()
            for d in (1, 2, 3):
                z_out(d, n, g).wait_send()
        store_wide(g).wait()
        store_slim(0, g).wait()
        store_slim(1, g).wait()
        return carry

    lax.fori_loop(0, KVH, drain, 0)


def publish(gq_in, gk_in, gv_in, gq_out, gk_out, gv_out, wide, slim, in_sem, out_sem):
    loads, stores = [], []
    for n in range(8):
        rows = pl.ds(n * 16, 16)
        loads.append(pltpu.make_async_copy(gq_in.at[rows], wide.at[rows], in_sem.at[n]))
        stores.append(pltpu.make_async_copy(wide.at[rows], gq_out.at[rows], out_sem.at[n]))
    for n, (src, dst) in enumerate(((gk_in, gk_out), (gv_in, gv_out))):
        loads.append(pltpu.make_async_copy(src, slim.at[n], in_sem.at[8 + n]))
        stores.append(pltpu.make_async_copy(slim.at[n], dst, out_sem.at[8 + n]))
    for load in loads:
        load.start()
    for load, store in zip(loads, stores):
        load.wait()
        store.start()
    for store in stores:
        store.wait()


def shards(queries, keys, values, outputs, grad_out, lse_saved, doc_lengths):
    half, full = jnp.bfloat16, jnp.float32
    anywhere = pl.BlockSpec(memory_space=pl.ANY)
    vmem = pl.BlockSpec(memory_space=pltpu.VMEM)
    grads = pl.pallas_call(
        kernel,
        out_shape=(
            jax.ShapeDtypeStruct((ROWS, HEADS * HDIM), half),
            jax.ShapeDtypeStruct((ROWS, KVH * HDIM), half),
            jax.ShapeDtypeStruct((ROWS, KVH * HDIM), half),
        ),
        in_specs=[anywhere] * 5 + [vmem, pl.BlockSpec(memory_space=pltpu.SMEM)],
        out_specs=(anywhere,) * 3,
        scratch_shapes=[
            pltpu.VMEM((2, KVH, SLOTS, ROWS, HDIM), half),
            pltpu.VMEM((2, KVH, 3, ROWS, HDIM), half),
            pltpu.VMEM((2, KVH, 6, ROWS, HDIM), full),
            pltpu.VMEM((2, KVH, 3, ROWS, HDIM), half),
            pltpu.VMEM((2, 2, KVH, ROWS, HDIM), half),
            pltpu.VMEM((2, KVH, 3, ROWS, HDIM), half),
            pltpu.VMEM((3, 2, KVH, ROWS, HDIM), half),
            pltpu.VMEM((2, KVH, 2, ROWS, HDIM), half),
            pltpu.VMEM((2, KVH, 2, ROWS, HDIM), half),
            pltpu.VMEM((KVH, ROWS, WIDE), half),
            pltpu.VMEM((KVH, ROWS, WIDE), half),
            pltpu.VMEM((KVH, ROWS, WIDE), half),
            pltpu.VMEM((KVH, ROWS, WIDE), half),
            pltpu.VMEM((WIDE, HDIM), half),
            pltpu.VMEM((WIDE, HDIM), half),
            pltpu.VMEM((HEADS, ROWS), full),
            pltpu.VMEM((1, WIDE), full),
            pltpu.VMEM((1, WIDE), full),
            pltpu.VMEM((KEYS, ROWS), full),
            pltpu.VMEM((HDIM, WIDE), full),
            pltpu.VMEM((2, KVH, ROWS, HDIM), half),
            pltpu.SemaphoreType.DMA((3, KVH)),
            pltpu.SemaphoreType.DMA((2, KVH)),
            pltpu.SemaphoreType.DMA((KVH,)),
            pltpu.SemaphoreType.DMA((2, KVH)),
            pltpu.SemaphoreType.DMA((27, KVH)),
            pltpu.SemaphoreType.DMA((27, KVH)),
        ],
        compiler_params=pltpu.CompilerParams(
            collective_id=0,
            has_side_effects=True,
            vmem_limit_bytes=62 * 1024 * 1024,
        ),
        name="attention_backward",
    )(queries, keys, values, outputs, grad_out, lse_saved.T, doc_lengths)
    return pl.pallas_call(
        publish,
        out_shape=(
            jax.ShapeDtypeStruct((ROWS, HEADS * HDIM), half),
            jax.ShapeDtypeStruct((ROWS, KVH * HDIM), half),
            jax.ShapeDtypeStruct((ROWS, KVH * HDIM), half),
        ),
        in_specs=[anywhere] * 3,
        out_specs=(anywhere,) * 3,
        scratch_shapes=[
            pltpu.VMEM((ROWS, HEADS * HDIM), half),
            pltpu.VMEM((2, ROWS, KVH * HDIM), half),
            pltpu.SemaphoreType.DMA((10,)),
            pltpu.SemaphoreType.DMA((10,)),
        ],
        name="publish",
    )(*grads)


def solution(mesh):
    placed = P(("packs", "seq"), None)
    return jax.shard_map(
        shards,
        mesh=mesh,
        in_specs=(placed,) * 6 + (P("packs"),),
        out_specs=(placed,) * 3,
        check_vma=False,
    )
```

```python
import functools

import jax
import jax.numpy as jnp
from jax import lax
from jax.experimental import pallas as pl
from jax.experimental.pallas import tpu as pltpu
from jax.sharding import PartitionSpec as P

HEADS = 64
KVH = 8
HDIM = 128
GROUP = HEADS // KVH
ROWS = 128
WIDE = GROUP * HDIM
SIDE = 4
SLOTS = 9
KEYS = SLOTS * ROWS
DOCS = 8
LAG = (1, 2, 3, 4, 5)
LOOK = 3
HEAVY = ((0, 0), (0, 1), (1, 0), (1, 1))
LIGHT = ((0, 0),)
LEAD = 2
TAIL = 2
SCALE = 1.0 / HDIM**0.5
LOG2E = 1.4426950408889634
MESH = pl.DeviceIdType.MESH


def kernel(
    q_hbm,
    k_hbm,
    v_hbm,
    o_hbm,
    go_hbm,
    lse_ref,
    doc_ref,
    gq_hbm,
    gk_hbm,
    gv_hbm,
    kvw,
    part,
    acc,
    partr,
    crossr,
    side,
    sider,
    prev,
    prevr,
    qb,
    gb,
    ob,
    gqb,
    qs,
    gs,
    lse_t,
    nlse,
    delta,
    bias,
    dq,
    slim,
    in_sem,
    kv_sem,
    out_sem,
    slim_sem,
    send_sem,
    recv_sem,
):
    me = lax.axis_index("seq")
    y, z = me // SIDE, lax.rem(me, SIDE)

    def at(dy, dz):
        return lax.rem(y + dy + SIDE, SIDE) * SIDE + lax.rem(z + dz + SIDE, SIDE)

    def remote(src, dst, kind, g, target):
        return pltpu.make_async_remote_copy(
            src_ref=src,
            dst_ref=dst,
            send_sem=send_sem.at[kind, g],
            recv_sem=recv_sem.at[kind, g],
            device_id={"seq": target},
            device_id_type=MESH,
        )

    firsts = (jnp.where(z < 3, 0, 1), jnp.where(z < 2, 0, 1), jnp.where(z < 1, 0, 1))

    def y_in(j, g):
        return remote(kvw.at[:, g, j - 1], kvw.at[:, g, j], j - 1, g, at(1, 0))

    def z_in(d, g):
        return remote(kvw.at[:, g, firsts[d - 1]], kvw.at[:, g, 2 + d], 1 + d, g, at(0, d))

    seconds = (firsts[0] + 1, firsts[2] + 1)

    def cross_in(n, e, g):
        return remote(
            kvw.at[n, g, seconds[e]], kvw.at[n, g, 6 + 2 * e], 5 + 2 * n + e, g, at(0, 1 - 2 * e)
        )

    def cross_out(n, e, g):
        return remote(
            part.at[n, g, 2 * e], crossr.at[n, e, g], 9 + 2 * n + e, g, at(0, 2 * e - 1)
        )

    def span(n, cross):
        return int((n, 0) in cross), 3 - int((n, 1) in cross)

    def row_in(n, cross, g):
        low, high = span(n, cross)
        src, dst = pl.ds(3 + low, high - low), pl.ds(6 + low, high - low)
        return remote(kvw.at[n, g, src], kvw.at[n, g, dst], 13 + n, g, at(1, 0))

    def row_out(n, cross, g):
        low, high = span(n, cross)
        rows = pl.ds(low, high - low)
        return remote(part.at[n, g, rows], partr.at[n, g, rows], 15 + n, g, at(-1, 0))

    def by_load(heavy, body):
        @pl.when(heavy)
        def _():
            body(HEAVY)

        @pl.when(jnp.logical_not(heavy))
        def _():
            body(LIGHT)

    def in_load(g, body):
        by_load(g < LEAD, body)

    def out_load(g, body):
        by_load(g >= KVH - TAIL, body)

    def z_out(d, n, g):
        return remote(
            side.at[n, g, d - 1], sider.at[d - 1, n, g], 14 + 3 * n + d + 2, g, at(0, -d)
        )

    def y_out(j, n, g):
        return remote(prev.at[n, g, j], prevr.at[n, g, j], 23 + 2 * j + n, g, at(-1, 0))

    def columns(g, width):
        return pl.ds(pl.multiple_of(g * width, width), width)

    def load_kv(n, g):
        src = (k_hbm, v_hbm)[n]
        return pltpu.make_async_copy(
            src.at[:, columns(g, HDIM)], kvw.at[n, g, 0], kv_sem.at[n, g]
        )

    def load_wide(n, g):
        src, dst = ((q_hbm, qb), (go_hbm, gb), (o_hbm, ob))[n]
        return pltpu.make_async_copy(src.at[:, columns(g, WIDE)], dst.at[g], in_sem.at[n, g])

    def store_slim(n, g):
        dst = (gk_hbm, gv_hbm)[n]
        return pltpu.make_async_copy(slim.at[n, g], dst.at[:, columns(g, HDIM)], slim_sem.at[n, g])

    def store_wide(g):
        return pltpu.make_async_copy(gqb.at[g], gq_hbm.at[:, columns(g, WIDE)], out_sem.at[g])

    for g in range(KVH):
        load_kv(0, g).start()
        load_kv(1, g).start()
    for g in range(KVH):
        for n in range(3):
            load_wide(n, g).start()

    barrier = pltpu.get_barrier_semaphore()
    for dy, dz in ((1, 0), (2, 0), (3, 0), (0, 1), (0, 2), (0, 3)):
        pl.semaphore_signal(
            barrier, inc=1, device_id={"seq": at(dy, dz)}, device_id_type=MESH
        )
    pl.semaphore_wait(barrier, 6)

    def send_first(g):
        load_kv(0, g).wait()
        load_kv(1, g).wait()
        y_in(1, g).start()

    for g in range(LOOK):
        send_first(g)

    lse_t[...] = lse_ref[...] * LOG2E
    time = lax.broadcasted_iota(jnp.int32, (1, ROWS), 1) + me * ROWS
    begin = jnp.zeros((1, ROWS), jnp.int32)
    bound = doc_ref[0]
    for n in range(1, DOCS):
        begin = jnp.where(time >= bound, bound, begin)
        bound = bound + doc_ref[n]
    for slot in range(SLOTS):
        back = (0, 4, 8, 1, 2, 3, 5, 6, 7)[slot]
        row = lax.rem(me - back + SIDE * SIDE, SIDE * SIDE)
        keys_at = lax.broadcasted_iota(jnp.int32, (ROWS, ROWS), 0) + row * ROWS
        seen = (keys_at <= time) & (keys_at >= begin)
        bias[pl.ds(slot * ROWS, ROWS), :] = jnp.where(seen, 0.0, -1e30)

    def prepare(g):
        for n in range(3):
            load_wide(n, g).wait()
        logs = lse_t[pl.ds(pl.multiple_of(g * GROUP, GROUP), GROUP), :]
        for h in range(GROUP):
            cut = slice(h * HDIM, (h + 1) * HDIM)
            query, gout = qb[g, :, cut], gb[g, :, cut]
            qs[cut, :] = query
            gs[cut, :] = gout
            product = ob[g, :, cut].astype(jnp.float32) * gout.astype(jnp.float32)
            delta[:, cut] = jnp.sum(product.T, axis=0, keepdims=True)
            nlse[:, cut] = logs[h : h + 1, :]

    def attend(g, low, high):
        rows = (high - low) * ROWS
        k = kvw[0, g, low:high].reshape(rows, HDIM)
        v = kvw[1, g, low:high].reshape(rows, HDIM)
        nt = (((1,), (1,)), ((), ()))
        tn = (((0,), (0,)), ((), ()))
        scores = lax.dot_general(k, qs[...], nt, preferred_element_type=jnp.float32)
        hidden = jnp.concatenate([bias[low * ROWS : high * ROWS, :]] * GROUP, axis=1)
        prob = jnp.exp2(scores * (SCALE * LOG2E) - nlse[...] + hidden)
        grad_prob = lax.dot_general(v, gs[...], nt, preferred_element_type=jnp.float32)
        grad_score = (prob * (grad_prob - delta[...])).astype(jnp.bfloat16)
        half = prob.astype(jnp.bfloat16)
        grad_v = jnp.dot(half, gs[...], preferred_element_type=jnp.float32)
        grad_k = jnp.dot(grad_score, qs[...], preferred_element_type=jnp.float32) * SCALE
        grad_q = lax.dot_general(k, grad_score, tn, preferred_element_type=jnp.float32)
        shape = (high - low, ROWS, HDIM)
        return grad_q, grad_k.reshape(shape), grad_v.reshape(shape)

    def near(g):
        @pl.when(g > 0)
        def _():
            prepare(g)

        grad_q, grad_k, grad_v = attend(g, 0, 6)
        dq[...] = grad_q
        acc[0, g] = grad_k
        acc[1, g] = grad_v

    def distant(g, leave):
        rows = 3 * ROWS
        k = kvw[0, g, 6:9].reshape(rows, HDIM)
        v = kvw[1, g, 6:9].reshape(rows, HDIM)
        nt = (((1,), (1,)), ((), ()))
        tn = (((0,), (0,)), ((), ()))
        shape = (3, ROWS, HDIM)
        scores = lax.dot_general(k, qs[...], nt, preferred_element_type=jnp.float32)
        hidden = jnp.concatenate([bias[6 * ROWS :, :]] * GROUP, axis=1)
        prob = jnp.exp2(scores * (SCALE * LOG2E) - nlse[...] + hidden)
        half = prob.astype(jnp.bfloat16)
        grad_v = jnp.dot(half, gs[...], preferred_element_type=jnp.float32)
        part[1, g] = grad_v.reshape(shape).astype(jnp.bfloat16)
        leave(1)
        grad_prob = lax.dot_general(v, gs[...], nt, preferred_element_type=jnp.float32)
        grad_score = (prob * (grad_prob - delta[...])).astype(jnp.bfloat16)
        grad_k = jnp.dot(grad_score, qs[...], preferred_element_type=jnp.float32) * SCALE
        part[0, g] = grad_k.reshape(shape).astype(jnp.bfloat16)
        leave(0)
        dq[...] += lax.dot_general(k, grad_score, tn, preferred_element_type=jnp.float32)

    def finish(g):
        for h in range(GROUP):
            cut = slice(h * HDIM, (h + 1) * HDIM)
            gqb[g, :, cut] = (dq[:, cut].T * SCALE).astype(jnp.bfloat16)
        store_wide(g).start()

    def step(s, carry):
        @pl.when(s < KVH)
        def _():
            y_in(1, s).wait_recv()
            y_in(2, s).start()
            for d in (2, 1, 3):
                z_in(d, s).start()

            @pl.when(s < KVH - LOOK)
            def _():
                send_first(s + LOOK)

        @pl.when((s >= LAG[0]) & (s < KVH + LAG[0]))
        def _():
            g = s - LAG[0]
            y_in(2, g).wait_recv()

            def send(cross):
                for n, e in cross:
                    cross_in(n, e, g).start()
                for d in (1, 3, 2):
                    z_in(d, g).wait_recv()
                row_in(0, cross, g).start()
                row_in(1, cross, g).start()

            in_load(g, send)

        @pl.when((s >= LAG[1]) & (s < KVH + LAG[1]))
        def _():
            g = s - LAG[1]

            def arrive(cross):
                for n, e in cross:
                    cross_in(n, e, g).wait_recv()
                for n in range(2):
                    row_in(n, cross, g).wait_recv()

            def leave(n):
                def send(cross):
                    for m, e in cross:
                        if m == n:
                            cross_out(n, e, g).start()
                    row_out(n, cross, g).start()

                out_load(g, send)

            in_load(g, arrive)
            distant(g, leave)

        @pl.when((s >= LAG[2]) & (s < KVH + LAG[2]))
        def _():
            g = s - LAG[2]

            def collect(cross):
                for n in (1, 0):
                    for m, e in cross:
                        if m == n:
                            cross_out(n, e, g).wait_recv()
                            acc[n, g, seconds[e]] += crossr[n, e, g].astype(jnp.float32)
                    prev[n, g, 1] = acc[n, g, 2].astype(jnp.bfloat16)
                    y_out(1, n, g).start()
                    row_out(n, cross, g).wait_recv()
                    low, high = span(n, cross)
                    acc[n, g, 3 + low : 3 + high] += partr[n, g, low:high].astype(jnp.float32)
                    side[n, g] = acc[n, g, 3:6].astype(jnp.bfloat16)
                    for d in (2, 1, 3):
                        z_out(d, n, g).start()

            out_load(g, collect)

        @pl.when((s >= LAG[1]) & (s < KVH + LAG[1]))
        def _():
            finish(s - LAG[1])

        @pl.when((s >= LAG[1] - 1) & (s < KVH + LAG[1] - 1))
        def _():
            near(s - LAG[1] + 1)

        @pl.when((s >= LAG[3]) & (s < KVH + LAG[3]))
        def _():
            g = s - LAG[3]
            for n in (1, 0):
                y_out(1, n, g).wait_recv()
                acc[n, g, 1] += prevr[n, g, 1].astype(jnp.float32)
                for d in (1, 3, 2):
                    z_out(d, n, g).wait_recv()
                    acc[n, g, firsts[d - 1]] += sider[d - 1, n, g].astype(jnp.float32)
                prev[n, g, 0] = acc[n, g, 1].astype(jnp.bfloat16)
                y_out(0, n, g).start()

        @pl.when(s >= LAG[4])
        def _():
            g = s - LAG[4]
            for n in range(2):
                y_out(0, n, g).wait_recv()
                total = acc[n, g, 0] + prevr[n, g, 0].astype(jnp.float32)
                slim[n, g] = total.astype(jnp.bfloat16)
                store_slim(n, g).start()

        return carry

    prepare(0)
    lax.fori_loop(0, KVH + LAG[4], step, 0)

    def drain(g, carry):
        def sent_in(cross):
            for n, e in cross:
                cross_in(n, e, g).wait_send()
            for n in range(2):
                row_in(n, cross, g).wait_send()

        def sent_out(cross):
            for n, e in cross:
                cross_out(n, e, g).wait_send()
            for n in range(2):
                row_out(n, cross, g).wait_send()

        in_load(g, sent_in)
        out_load(g, sent_out)
        for d in (1, 2, 3):
            z_in(d, g).wait_send()
        for n in range(2):
            y_in(n + 1, g).wait_send()
            for j in range(2):
                y_out(j, n, g).wait_send()
            for d in (1, 2, 3):
                z_out(d, n, g).wait_send()
        store_wide(g).wait()
        store_slim(0, g).wait()
        store_slim(1, g).wait()
        return carry

    lax.fori_loop(0, KVH, drain, 0)


def publish(gq_in, gk_in, gv_in, gq_out, gk_out, gv_out, wide, slim, in_sem, out_sem):
    loads, stores = [], []
    for n in range(8):
        rows = pl.ds(n * 16, 16)
        loads.append(pltpu.make_async_copy(gq_in.at[rows], wide.at[rows], in_sem.at[n]))
        stores.append(pltpu.make_async_copy(wide.at[rows], gq_out.at[rows], out_sem.at[n]))
    for n, (src, dst) in enumerate(((gk_in, gk_out), (gv_in, gv_out))):
        loads.append(pltpu.make_async_copy(src, slim.at[n], in_sem.at[8 + n]))
        stores.append(pltpu.make_async_copy(slim.at[n], dst, out_sem.at[8 + n]))
    for load in loads:
        load.start()
    for load, store in zip(loads, stores):
        load.wait()
        store.start()
    for store in stores:
        store.wait()


def shards(queries, keys, values, outputs, grad_out, lse_saved, doc_lengths):
    half, full = jnp.bfloat16, jnp.float32
    anywhere = pl.BlockSpec(memory_space=pl.ANY)
    vmem = pl.BlockSpec(memory_space=pltpu.VMEM)
    grads = pl.pallas_call(
        kernel,
        out_shape=(
            jax.ShapeDtypeStruct((ROWS, HEADS * HDIM), half),
            jax.ShapeDtypeStruct((ROWS, KVH * HDIM), half),
            jax.ShapeDtypeStruct((ROWS, KVH * HDIM), half),
        ),
        in_specs=[anywhere] * 5 + [vmem, pl.BlockSpec(memory_space=pltpu.SMEM)],
        out_specs=(anywhere,) * 3,
        scratch_shapes=[
            pltpu.VMEM((2, KVH, SLOTS, ROWS, HDIM), half),
            pltpu.VMEM((2, KVH, 3, ROWS, HDIM), half),
            pltpu.VMEM((2, KVH, 6, ROWS, HDIM), full),
            pltpu.VMEM((2, KVH, 3, ROWS, HDIM), half),
            pltpu.VMEM((2, 2, KVH, ROWS, HDIM), half),
            pltpu.VMEM((2, KVH, 3, ROWS, HDIM), half),
            pltpu.VMEM((3, 2, KVH, ROWS, HDIM), half),
            pltpu.VMEM((2, KVH, 2, ROWS, HDIM), half),
            pltpu.VMEM((2, KVH, 2, ROWS, HDIM), half),
            pltpu.VMEM((KVH, ROWS, WIDE), half),
            pltpu.VMEM((KVH, ROWS, WIDE), half),
            pltpu.VMEM((KVH, ROWS, WIDE), half),
            pltpu.VMEM((KVH, ROWS, WIDE), half),
            pltpu.VMEM((WIDE, HDIM), half),
            pltpu.VMEM((WIDE, HDIM), half),
            pltpu.VMEM((HEADS, ROWS), full),
            pltpu.VMEM((1, WIDE), full),
            pltpu.VMEM((1, WIDE), full),
            pltpu.VMEM((KEYS, ROWS), full),
            pltpu.VMEM((HDIM, WIDE), full),
            pltpu.VMEM((2, KVH, ROWS, HDIM), half),
            pltpu.SemaphoreType.DMA((3, KVH)),
            pltpu.SemaphoreType.DMA((2, KVH)),
            pltpu.SemaphoreType.DMA((KVH,)),
            pltpu.SemaphoreType.DMA((2, KVH)),
            pltpu.SemaphoreType.DMA((27, KVH)),
            pltpu.SemaphoreType.DMA((27, KVH)),
        ],
        compiler_params=pltpu.CompilerParams(
            collective_id=0,
            has_side_effects=True,
            vmem_limit_bytes=62 * 1024 * 1024,
        ),
        name="attention_backward",
    )(queries, keys, values, outputs, grad_out, lse_saved.T, doc_lengths)
    return pl.pallas_call(
        publish,
        out_shape=(
            jax.ShapeDtypeStruct((ROWS, HEADS * HDIM), half),
            jax.ShapeDtypeStruct((ROWS, KVH * HDIM), half),
            jax.ShapeDtypeStruct((ROWS, KVH * HDIM), half),
        ),
        in_specs=[anywhere] * 3,
        out_specs=(anywhere,) * 3,
        scratch_shapes=[
            pltpu.VMEM((ROWS, HEADS * HDIM), half),
            pltpu.VMEM((2, ROWS, KVH * HDIM), half),
            pltpu.SemaphoreType.DMA((10,)),
            pltpu.SemaphoreType.DMA((10,)),
        ],
        name="publish",
    )(*grads)


def solution(mesh):
    placed = P(("packs", "seq"), None)
    return jax.shard_map(
        shards,
        mesh=mesh,
        in_specs=(placed,) * 6 + (P("packs"),),
        out_specs=(placed,) * 3,
        check_vma=False,
    )
```
